768 devices in a mesh: band: 12 (over z_lo, core), col: 64 (over x, y, z_hi).
Axes of the slice: x: 4, y: 8, z: 12 (z_hi: 2, z_lo: 6; z = z_hi * 6 + z_lo), core: 2. Of those that a mesh axis runs over, the one named last changes fastest.
Arguments:
- adjoint_tend: bfloat16 [64, 40, 12, 5120], P('col', None, 'band'), may hold values from -6 to 6
- trajectory: bfloat16 [40, 12, 5120], P(None, 'band', 'col'), may hold values from -3 to 3
- coupling: bfloat16 [40, 40], replicated, may hold values from -1 to 1
- row_lat: int32 [12], P('band'), may hold values from 0 to 2559, as said below
- row_points: int32 [12], P('band'), may hold values from 20 to 5120, as said below
- wave_order: int32 [768], replicated, may hold values from 0 to 767, each once
Outputs:
- spectra: bfloat16 [64, 2, 40, 12, 768], P('col', None, None, None, 'band')
The draws below stay inside these ranges and needn't reach their ends.
Inputs may be any that keep to these rules, and one draw needn't show every extreme that they name: `row_lat`: latitude rows are counted from the north pole. `row_points`: the row of latitude index i has min(20 + 4 d, 5120) points, d = min(i, 2559 - i), placed at point indices 0 to that number minus one; the rest of the row slot is unused.
All inputs are finite; a program needn't handle non-finite values.
Results may differ from the reference program's by a relative error of at most 0.0055.
Values may be sent and summed in bfloat16 or wider, within the bound.
A program may use at most 64 MiB of HBM per device.

```python
import math
import jax
import jax.numpy as jnp
from jax import lax

LEVELS = 8
COLUMN_VARS = 40
ROW_SLOTS = 5120
WAVES = 768
LATITUDES = 2560
ROWS = 12
MEMBERS = 64


def latitude_rows(key):
    picked = jax.random.randint(jax.random.fold_in(key, 11), (ROWS,), 0, LATITUDES)
    shuffled = jax.random.permutation(jax.random.fold_in(key, 12), ROWS)
    slots = jnp.arange(ROWS, dtype=jnp.int32)
    equator_slot = shuffled[0]
    south_slot = shuffled[1]
    north_slot = shuffled[2]
    values = jnp.where(slots == north_slot, 0, picked)
    values = jnp.where(slots == south_slot, LATITUDES - 1, values)
    values = jnp.where(slots == equator_slot, LATITUDES // 2, values)
    return values.astype(jnp.int32)


def draw_row_lat(key, part):
    return latitude_rows(key)


def draw_row_points(key, part):
    latitude = latitude_rows(key)
    distance = jnp.minimum(latitude, LATITUDES - 1 - latitude)
    return jnp.minimum(20 + 4 * distance, ROW_SLOTS).astype(jnp.int32)


def levels(own_key, dims, split, least, top_value):
    def one(dim, blocks):
        heights = jax.random.uniform(jax.random.fold_in(jax.random.fold_in(own_key, 6), dim), (blocks,), jnp.float32, least / len(split), top_value / len(split))
        return jnp.repeat(jnp.exp(heights), dims[dim] // blocks).reshape((-1,) + (1,) * (len(dims) - dim - 1))

    factor_of = one(*split[0])
    for cut in split[1:]:
        factor_of = factor_of * one(*cut)
    return factor_of


def centred(key, shape, deviation, most, split=(), held_as=jnp.bfloat16):
    entries = jax.random.normal(key, shape, jnp.float32) * deviation
    if len(split) > 0:
        entries = levels(key, shape, split, -0.22, 0.18) * entries
    return jnp.clip(entries, min=-most, max=most).astype(held_as)


def setup_inputs(seed: int = 0) -> dict:
    key_of = jax.random.split(jax.random.key(seed), 7)
    return {
        "adjoint_tend": centred(key_of[0], (MEMBERS, COLUMN_VARS, ROWS, ROW_SLOTS), 1.0, 6.0, ((0, 64), (2, 12))),
        "trajectory": centred(key_of[1], (COLUMN_VARS, ROWS, ROW_SLOTS), 0.5, 3.0, ((1, 12), (2, 64))),
        "coupling": centred(key_of[2], (COLUMN_VARS, COLUMN_VARS), COLUMN_VARS ** -0.5, 1.0),
        "row_lat": draw_row_lat(jax.random.fold_in(key_of[6], 71), 0),
        "row_points": draw_row_points(jax.random.fold_in(key_of[6], 71), 0),
        "wave_order": jax.random.permutation(key_of[5], WAVES).astype(jnp.int32),
    }


def latitude_factor(row_lat):
    ratio = (2.0 * row_lat.astype(jnp.float32) + 1.0) / LATITUDES
    return jnp.sin(0.5 * math.pi * (1.0 - ratio))

def grid_adjoint(tend_block, traj_block, coupling, coriolis, row_points, first_point):
    width = tend_block.shape[3]
    traj_wide = traj_block.astype(jnp.float32)
    coupling_wide = coupling.astype(jnp.float32)
    driven = jnp.einsum('ab,brp->arp', coupling_wide, traj_wide, precision=lax.Precision.HIGHEST)
    tend_wide = tend_block.astype(jnp.float32)
    weighted = tend_wide * (1.0 + traj_wide)[None]
    backed = jnp.einsum('ab,karp->kbrp', coupling_wide, weighted, precision=lax.Precision.HIGHEST)
    total = backed + tend_wide * driven[None]
    turning = coriolis[None, None, :, None]
    eastward = tend_wide[:, :LEVELS]
    northward = tend_wide[:, LEVELS:2 * LEVELS]
    total = jnp.concatenate([total[:, :LEVELS] - turning * northward, total[:, LEVELS:2 * LEVELS] + turning * eastward, total[:, 2 * LEVELS:]], axis=1)
    places = first_point + jnp.arange(width, dtype=jnp.int32)
    keep = places[None, :] < row_points[:, None]
    return jnp.where(keep[None, None], total, 0.0).astype(jnp.bfloat16)

def wave_table(points, waves, width):
    places = jnp.arange(width, dtype=jnp.int32)
    phase = places[:, None] * waves[None, :] % points
    angle = phase.astype(jnp.float32) * (2.0 * math.pi) / points.astype(jnp.float32)
    keep = (2 * waves < points)[None, :]
    cosine = jnp.where(keep, jnp.cos(angle), 0.0)
    sine = jnp.where(keep, -jnp.sin(angle), 0.0)
    return jnp.concatenate([cosine, sine], axis=1).astype(jnp.bfloat16)

def reference(adjoint_tend, trajectory, coupling, row_lat, row_points, wave_order):
    coriolis = latitude_factor(row_lat)

    def one_row(row_index):
        tend_row = lax.dynamic_slice_in_dim(adjoint_tend, row_index, 1, 2)
        traj_row = lax.dynamic_slice_in_dim(trajectory, row_index, 1, 1)
        turn_row = lax.dynamic_slice_in_dim(coriolis, row_index, 1, 0)
        count_row = lax.dynamic_slice_in_dim(row_points, row_index, 1, 0)
        grid = grid_adjoint(tend_row, traj_row, coupling, turn_row, count_row, 0)
        table = wave_table(count_row[0], wave_order, ROW_SLOTS)
        flat = grid.reshape(MEMBERS * COLUMN_VARS, ROW_SLOTS)
        coeffs = jnp.dot(flat.astype(jnp.float32), table.astype(jnp.float32), precision=lax.Precision.HIGHEST)
        coeffs = coeffs / jnp.sqrt(count_row[0].astype(jnp.float32))
        return coeffs.astype(jnp.bfloat16).reshape(MEMBERS, COLUMN_VARS, 2, WAVES)
    rows_out = lax.map(one_row, jnp.arange(ROWS, dtype=jnp.int32))
    return jnp.transpose(rows_out, (1, 3, 2, 0, 4))
```

```python
import jax
import jax.numpy as jnp
from jax import lax
from jax.experimental import pallas as pl
from jax.experimental.pallas import tpu as pltpu
from jax.sharding import PartitionSpec as P

LEVELS = 8
LATITUDES = 2560
VARS = 40
POINTS = 5120
PIECE = 80
COLS = 64
BANDS = 12
OWN_WAVES = 64
LANES = 2 * BANDS * OWN_WAVES
FINE = 256
COARSE = POINTS // FINE
SINE = (6.283185005187988, -41.34165573120117, 81.60100555419922, -76.5497817993164, 39.536705017089844)


def sine_turns(v):
    u = v * v
    p = jnp.full_like(u, SINE[-1])
    for c in SINE[-2::-1]:
        p = p * u + c
    return p * v


def cosine_turns(t):
    v = 0.25 - jnp.abs(t)
    return sine_turns(jnp.maximum(v, -0.5 - v))


def turns(pm, n, rn):
    q = jnp.floor(pm * rn + 0.5)
    return (pm - q * n) * rn


def tables(pts_ref, waves_ref, fine_ref, a_ref, b_ref):
    points = pts_ref[0].astype(jnp.float32)
    lane = lax.broadcasted_iota(jnp.int32, (8, 128), 1)
    first_half = lane < 64
    n8 = jnp.full((8, 128), points, jnp.float32)
    rn8 = 1.0 / n8
    root8 = 1.0 / jnp.sqrt(n8)
    shift8 = jnp.where(first_half, 0.0, 0.25)
    sign8 = jnp.where(first_half, 1.0, -1.0)
    for tile in range(6):
        pair = jnp.broadcast_to(waves_ref[:, 128 * tile : 128 * tile + 128], (8, 128)).astype(jnp.float32)
        turned = pltpu.roll(pair, 64, 1)
        for odd in range(2):
            w8 = jnp.where(first_half, pair, turned) if odd == 0 else jnp.where(first_half, turned, pair)
            at = (2 * tile + odd) * 128
            scale = jnp.where(2.0 * w8 < n8, root8, 0.0)
            for k in range(3):
                p1 = lax.broadcasted_iota(jnp.int32, (8, 128), 0).astype(jnp.float32) + 8.0 * k
                t = turns(p1 * FINE * w8, n8, rn8)
                a_ref[8 * k : 8 * k + 8, at : at + 128] = scale * sign8 * cosine_turns(t)
                b_ref[8 * k : 8 * k + 8, at : at + 128] = -scale * cosine_turns(t - 0.25)
            wide = lambda v: jnp.broadcast_to(v[None], (FINE // 8, 8, 128)).reshape(FINE, 128)
            p0 = lax.broadcasted_iota(jnp.int32, (FINE, 128), 0).astype(jnp.float32)
            t = turns(p0 * wide(w8), wide(n8), wide(rn8))
            fine_ref[:, at : at + 128] = cosine_turns(t - wide(shift8)).astype(jnp.bfloat16)


def joined(pieces):
    lane = lax.broadcasted_iota(jnp.int32, (VARS, 128), 1)
    tiles = [None] * 5
    for j, piece in enumerate(pieces):
        tile, at = divmod(PIECE * j, 128)
        turned = piece if at == 0 else pltpu.roll(piece, at, 1)
        tiles[tile] = turned if tiles[tile] is None else jnp.where(lane < at, tiles[tile], turned)
        if at + PIECE > 128:
            tiles[tile + 1] = turned
    return jnp.concatenate(tiles, axis=1)


def column(lat_ref, pts_ref, tend_ref, piece_of, coup_ref, x_ref):
    ratio = (2.0 * jnp.full((8, 128), lat_ref[0].astype(jnp.float32)) + 1.0) / LATITUDES
    turning = jnp.tile(sine_turns(0.25 - 0.25 * ratio), (1, 5))
    coup = coup_ref[...]
    back = coup.astype(jnp.float32).T.astype(jnp.bfloat16)
    back2 = jnp.concatenate([back, back], axis=1)
    points = pts_ref[0]
    place = lax.broadcasted_iota(jnp.int32, (VARS, 640), 1)

    def run(g):
        at = g * 640
        traj = joined([piece_of(8 * g + j).astype(jnp.float32) for j in range(8)])
        tend = tend_ref[:, pl.ds(pl.multiple_of(at, 128), 640)].astype(jnp.float32)
        driven = jnp.dot(coup, traj.astype(jnp.bfloat16), preferred_element_type=jnp.float32)
        weighted = tend * (1.0 + traj)
        high = weighted.astype(jnp.bfloat16).astype(jnp.float32)
        both = jnp.concatenate([high, weighted - high], axis=0).astype(jnp.bfloat16)
        backed = jnp.dot(back2, both, preferred_element_type=jnp.float32)
        total = backed + tend * driven
        total = jnp.concatenate(
            [
                total[:LEVELS] - turning * tend[LEVELS : 2 * LEVELS],
                total[LEVELS : 2 * LEVELS] + turning * tend[:LEVELS],
                total[2 * LEVELS :],
            ],
            axis=0,
        )
        return jnp.where(place < points - at, total, 0.0)

    def two_runs(i, carry):
        for half in range(2):
            total = run(2 * i + half)
            for k in range(5):
                tile = 5 * half + k
                x_ref[5 * i + tile // 2, :, 128 * (tile % 2) : 128 * (tile % 2) + 128] = total[:, 128 * k : 128 * k + 128]
        return carry

    lax.fori_loop(0, 4, two_runs, 0)


def transform(x_ref, x16_ref, fine_ref, a_ref, b_ref, put):
    x16_ref[...] = x_ref[...].reshape(COARSE * VARS, FINE).astype(jnp.bfloat16)

    def block(j, carry):
        at = pl.multiple_of(j * 256, 256)
        y = jnp.dot(x16_ref[...], fine_ref[:, pl.ds(at, 256)], preferred_element_type=jnp.float32)
        u = jnp.zeros((VARS, 256), jnp.float32)
        v = jnp.zeros((VARS, 256), jnp.float32)
        for p1 in range(COARSE):
            part = y[VARS * p1 : VARS * (p1 + 1)]
            u = u + part * a_ref[p1 : p1 + 1, pl.ds(at, 256)]
            v = v + part * b_ref[p1 : p1 + 1, pl.ds(at, 256)]
        for odd in range(2):
            half = slice(128 * odd, 128 * odd + 128)
            put(2 * j + odd, (u[:, half] + pltpu.roll(v[:, half], 64, 1)).astype(jnp.bfloat16))
        return carry

    lax.fori_loop(0, 6, block, 0)


def kernel(lat_ref, pts_ref, tend_ref, traj_ref, coup_ref, waves_ref, out_ref, fine_ref, a_ref, b_ref, x_ref, x16_ref):
    tables(pts_ref, waves_ref, fine_ref, a_ref, b_ref)

    def piece_of(j):
        return jnp.concatenate([traj_ref[j].astype(jnp.float32), jnp.zeros((VARS, 48), jnp.float32)], axis=1)

    column(lat_ref, pts_ref, tend_ref, piece_of, coup_ref, x_ref)

    def put(d, value):
        out_ref[d] = value

    transform(x_ref, x16_ref, fine_ref, a_ref, b_ref, put)


def body(adjoint_tend, trajectory, coupling, row_lat, row_points, wave_order):
    tend = adjoint_tend[0, :, 0, :]
    traj = lax.all_gather(trajectory[:, 0, :], "col", axis=0)
    vmem = pl.BlockSpec(memory_space=pltpu.VMEM)
    smem = pl.BlockSpec(memory_space=pltpu.SMEM)
    parts = pl.pallas_call(
        kernel,
        out_shape=jax.ShapeDtypeStruct((BANDS, VARS, 128), jnp.bfloat16),
        in_specs=[smem, smem, vmem, vmem, vmem, vmem],
        out_specs=vmem,
        scratch_shapes=[
            pltpu.VMEM((FINE, LANES), jnp.bfloat16),
            pltpu.VMEM((24, LANES), jnp.float32),
            pltpu.VMEM((24, LANES), jnp.float32),
            pltpu.VMEM((COARSE, VARS, FINE), jnp.float32),
            pltpu.VMEM((COARSE * VARS, FINE), jnp.bfloat16),
        ],
        compiler_params=pltpu.CompilerParams(vmem_limit_bytes=32 << 20),
    )(row_lat, row_points, tend, traj, coupling, wave_order.reshape(1, -1))
    parts = lax.all_to_all(parts, "band", split_axis=0, concat_axis=0, tiled=True)
    parts = parts.reshape(BANDS, VARS, 2, OWN_WAVES)
    return parts.transpose(2, 1, 0, 3)[None]


def solution(mesh):
    return jax.shard_map(
        body,
        mesh=mesh,
        in_specs=(
            P("col", None, "band", None),
            P(None, "band", "col"),
            P(),
            P("band"),
            P("band"),
            P(),
        ),
        out_specs=P("col", None, None, None, "band"),
        check_vma=False,
    )
```

```python
import jax
import jax.numpy as jnp
from jax import lax
from jax.experimental import pallas as pl
from jax.experimental.pallas import tpu as pltpu
from jax.sharding import PartitionSpec as P

LEVELS = 8
LATITUDES = 2560
VARS = 40
POINTS = 5120
WAVES = 768
PIECE = 80
MESH = pl.DeviceIdType.MESH
BANDS = 12
OWN_WAVES = 64
LANES = 2 * BANDS * OWN_WAVES
FINE = 256
COARSE = POINTS // FINE
SINE = (6.283185005187988, -41.34165573120117, 81.60100555419922, -76.5497817993164, 39.536705017089844)


def sine_turns(v):
    u = v * v
    p = jnp.full_like(u, SINE[-1])
    for c in SINE[-2::-1]:
        p = p * u + c
    return p * v


def cosine_turns(t):
    v = 0.25 - jnp.abs(t)
    return sine_turns(jnp.maximum(v, -0.5 - v))


def turns(pm, n, rn):
    q = jnp.floor(pm * rn + 0.5)
    return (pm - q * n) * rn


def tables(points, waves_ref, fine_ref, a_ref, b_ref, chosen):
    lane = lax.broadcasted_iota(jnp.int32, (8, 128), 1)
    first_half = lane < 64
    n8 = jnp.full((8, 128), points.astype(jnp.float32), jnp.float32)
    rn8 = 1.0 / n8
    root8 = 1.0 / jnp.sqrt(n8)
    shift8 = jnp.where(first_half, 0.0, 0.25)
    sign8 = jnp.where(first_half, 1.0, -1.0)
    row8 = lax.broadcasted_iota(jnp.int32, (8, 128), 0).astype(jnp.float32)
    for tile in chosen:
        pair = jnp.broadcast_to(waves_ref[pl.ds(128 * tile, 128)].reshape(1, 128), (8, 128)).astype(jnp.float32)
        turned = pltpu.roll(pair, 64, 1)
        for odd in range(2):
            w8 = jnp.where(first_half, pair, turned) if odd == 0 else jnp.where(first_half, turned, pair)
            at = (2 * tile + odd) * 128
            scale = jnp.where(2.0 * w8 < n8, root8, 0.0)
            for k in range(3):
                t = turns((row8 + 8.0 * k) * FINE * w8, n8, rn8)
                a_ref[8 * k : 8 * k + 8, at : at + 128] = scale * sign8 * cosine_turns(t)
                b_ref[8 * k : 8 * k + 8, at : at + 128] = -scale * cosine_turns(t - 0.25)
            wide = lambda v: jnp.broadcast_to(v[None], (FINE // 8, 8, 128)).reshape(FINE, 128)
            p0 = lax.broadcasted_iota(jnp.int32, (FINE, 128), 0).astype(jnp.float32)
            t = turns(p0 * wide(w8), wide(n8), wide(rn8))
            fine_ref[:, at : at + 128] = cosine_turns(t - wide(shift8)).astype(jnp.bfloat16)


def joined(pieces):
    lane = lax.broadcasted_iota(jnp.int32, (VARS, 128), 1)
    tiles = [None] * 5
    for j, piece in enumerate(pieces):
        tile, at = divmod(PIECE * j, 128)
        piece = jnp.concatenate([piece.astype(jnp.float32), jnp.zeros((VARS, 128 - PIECE), jnp.float32)], axis=1)
        turned = piece if at == 0 else pltpu.roll(piece, at, 1)
        tiles[tile] = turned if tiles[tile] is None else jnp.where(lane < at, tiles[tile], turned)
        if at + PIECE > 128:
            tiles[tile + 1] = turned
    return jnp.concatenate(tiles, axis=1).astype(jnp.bfloat16)


def column(latitude, points, tend_ref, traj_ref, coup_ref, x_ref, piece):
    ratio = (2.0 * jnp.full((8, 128), latitude.astype(jnp.float32)) + 1.0) / LATITUDES
    turning = jnp.tile(sine_turns(0.25 - 0.25 * ratio), (1, 5))
    coup = coup_ref[...]
    back = coup.astype(jnp.float32).T.astype(jnp.bfloat16)
    back2 = jnp.concatenate([back, back], axis=1)
    place = lax.broadcasted_iota(jnp.int32, (VARS, 640), 1)
    for half in range(2):
        at = (2 * piece + half) * 640
        traj16 = traj_ref[2 * piece + half]
        tend = tend_ref[:, pl.ds(pl.multiple_of(at, 128), 640)].astype(jnp.float32)
        driven = jnp.dot(coup, traj16, preferred_element_type=jnp.float32)
        weighted = tend * (1.0 + traj16.astype(jnp.float32))
        high = weighted.astype(jnp.bfloat16).astype(jnp.float32)
        both = jnp.concatenate([high, weighted - high], axis=0).astype(jnp.bfloat16)
        backed = jnp.dot(back2, both, preferred_element_type=jnp.float32)
        total = backed + tend * driven
        total = jnp.concatenate(
            [
                total[:LEVELS] - turning * tend[LEVELS : 2 * LEVELS],
                total[LEVELS : 2 * LEVELS] + turning * tend[:LEVELS],
                total[2 * LEVELS :],
            ],
            axis=0,
        )
        total = jnp.where(place < points - at, total, 0.0)
        for k in range(5):
            tile = 5 * half + k
            x_ref[5 * piece + tile // 2, :, 128 * (tile % 2) : 128 * (tile % 2) + 128] = total[:, 128 * k : 128 * k + 128]


def transform(x_ref, x16_ref, fine_ref, a_ref, b_ref, put):
    x16_ref[...] = x_ref[...].reshape(COARSE * VARS, FINE).astype(jnp.bfloat16)

    def block(j, carry):
        at = pl.multiple_of(j * 256, 256)
        y = jnp.dot(x16_ref[...], fine_ref[:, pl.ds(at, 256)], preferred_element_type=jnp.float32)
        u = jnp.zeros((VARS, 256), jnp.float32)
        v = jnp.zeros((VARS, 256), jnp.float32)
        for p1 in range(COARSE):
            part = y[VARS * p1 : VARS * (p1 + 1)]
            u = u + part * a_ref[p1 : p1 + 1, pl.ds(at, 256)]
            v = v + part * b_ref[p1 : p1 + 1, pl.ds(at, 256)]
        for odd in range(2):
            half = slice(128 * odd, 128 * odd + 128)
            put(2 * j + odd, (u[:, half] + pltpu.roll(v[:, half], 64, 1)).astype(jnp.bfloat16))
        return carry

    lax.fori_loop(0, 6, block, 0)


def kernel(
    tend_hbm, traj_hbm, coup_hbm, lat_hbm, pts_hbm, waves_hbm, out_ref,
    lat_ref, pts_ref, coup_ref, waves_ref, tend_ref, part_ref, line_ref, traj_ref, fine_ref, a_ref, b_ref, x_ref, x16_ref, send_ref,
    load_sem, own_sem, z_send, y_send, y_recv, x_send, x_recv, band_send, band_recv,
):
    band = lax.axis_index("band")
    col = lax.axis_index("col")
    x, y, z = col // 16, (col // 2) % 8, col % 2
    mine, other = 2 * y + z, 2 * y + 1 - z
    z_peer = (band, col + 1 - 2 * z)
    y_peers = [(band, 16 * x + 2 * ((y + s) % 8) + z) for s in range(1, 8)]
    x_peers = [(band, 16 * ((x + s) % 4) + 2 * y + z) for s in range(1, 4)]
    band_peers = [((band + s) % BANDS, col) for s in range(1, BANDS)]

    loads = [
        pltpu.make_async_copy(source, target, load_sem.at[i])
        for i, (source, target) in enumerate(
            [(pts_hbm, pts_ref), (waves_hbm, waves_ref), (lat_hbm, lat_ref), (coup_hbm, coup_ref), (tend_hbm, tend_ref)]
        )
    ]
    for load in loads:
        load.start()
    keep = pltpu.make_async_copy(traj_hbm, line_ref.at[mine], own_sem)
    keep.start()
    barrier = pltpu.get_barrier_semaphore()
    peers = [z_peer] + y_peers + x_peers + band_peers
    for peer in peers:
        pl.semaphore_signal(barrier, inc=1, device_id=peer, device_id_type=MESH)
    pl.semaphore_wait(barrier, len(peers))

    def to_line(source, slot, send_sem, peer):
        return pltpu.make_async_remote_copy(
            src_ref=source,
            dst_ref=line_ref.at[slot],
            send_sem=send_sem,
            recv_sem=y_recv.at[slot],
            device_id=peer,
            device_id_type=MESH,
        )

    across = to_line(traj_hbm, mine, z_send, z_peer)
    across.start()
    along = [to_line(traj_hbm, mine, y_send.at[0, s], peer) for s, peer in enumerate(y_peers)]
    for copy in along:
        copy.start()

    for load in loads[:2]:
        load.wait()
    points = pts_ref[0]
    tables(points, waves_ref, fine_ref, a_ref, b_ref, range(3))
    to_line(traj_hbm, other, z_send, z_peer).wait_recv()
    passed = [to_line(line_ref.at[other], other, y_send.at[1, s], peer) for s, peer in enumerate(y_peers)]
    for copy in passed:
        copy.start()
    tables(points, waves_ref, fine_ref, a_ref, b_ref, range(3, 6))
    keep.wait()
    for s in range(1, 8):
        for zz in range(2):
            to_line(traj_hbm, 2 * ((y + s) % 8) + zz, z_send, z_peer).wait_recv()

    spread = []
    for half in range(2):
        slot = 2 * x + half
        traj_ref[slot] = joined([line_ref[8 * half + j] for j in range(8)])
        for s, peer in enumerate(x_peers):
            copy = pltpu.make_async_remote_copy(
                src_ref=traj_ref.at[slot],
                dst_ref=traj_ref.at[slot],
                send_sem=x_send.at[half, s],
                recv_sem=x_recv.at[slot],
                device_id=peer,
                device_id_type=MESH,
            )
            copy.start()
            spread.append(copy)

    for load in loads[2:]:
        load.wait()
    for s in (0, 1, 3, 2):
        piece = (x + s) % 4
        if s > 0:
            for half in range(2):
                slot = 2 * piece + half
                pltpu.make_async_remote_copy(
                    src_ref=traj_ref.at[slot],
                    dst_ref=traj_ref.at[slot],
                    send_sem=x_send.at[half, 0],
                    recv_sem=x_recv.at[slot],
                    device_id=x_peers[0],
                    device_id_type=MESH,
                ).wait_recv()
        column(lat_ref[0], points, tend_ref, traj_ref, coup_ref, x_ref, piece)

    def put(d, value):
        send_ref[d] = value

    transform(x_ref, x16_ref, fine_ref, a_ref, b_ref, put)
    part_ref[band] = send_ref[band]

    def to_band(s, peer):
        return pltpu.make_async_remote_copy(
            src_ref=send_ref.at[peer[0]],
            dst_ref=part_ref.at[band],
            send_sem=band_send.at[s],
            recv_sem=band_recv.at[band],
            device_id=peer,
            device_id_type=MESH,
        )

    crossed = [to_band(s, peer) for s, peer in enumerate(band_peers)]
    for copy in crossed:
        copy.start()
    for s in range(1, BANDS):
        source = (band + s) % BANDS
        pltpu.make_async_remote_copy(
            src_ref=send_ref.at[source],
            dst_ref=part_ref.at[source],
            send_sem=band_send.at[0],
            recv_sem=band_recv.at[source],
            device_id=band_peers[0],
            device_id_type=MESH,
        ).wait_recv()
    for row in range(BANDS):
        both = part_ref[row].astype(jnp.float32)
        out_ref[0, row] = both[:, :OWN_WAVES].astype(jnp.bfloat16)
        out_ref[1, row] = both[:, OWN_WAVES:].astype(jnp.bfloat16)
    for copy in [across] + along + passed + spread + crossed:
        copy.wait_send()


def body(adjoint_tend, trajectory, coupling, row_lat, row_points, wave_order):
    vmem, smem, dma = pltpu.VMEM, pltpu.SMEM, pltpu.SemaphoreType.DMA
    spectra = pl.pallas_call(
        kernel,
        out_shape=jax.ShapeDtypeStruct((2, BANDS, VARS, OWN_WAVES), jnp.bfloat16),
        in_specs=[pl.BlockSpec(memory_space=pltpu.HBM)] * 6,
        out_specs=pl.BlockSpec(memory_space=vmem),
        scratch_shapes=[
            smem((1,), jnp.int32),
            smem((1,), jnp.int32),
            vmem((VARS, VARS), jnp.bfloat16),
            vmem((WAVES,), jnp.int32),
            vmem((VARS, POINTS), jnp.bfloat16),
            vmem((BANDS, VARS, 128), jnp.bfloat16),
            vmem((16, VARS, PIECE), jnp.bfloat16),
            vmem((8, VARS, 640), jnp.bfloat16),
            vmem((FINE, LANES), jnp.bfloat16),
            vmem((24, LANES), jnp.float32),
            vmem((24, LANES), jnp.float32),
            vmem((COARSE, VARS, FINE), jnp.float32),
            vmem((COARSE * VARS, FINE), jnp.bfloat16),
            vmem((BANDS, VARS, 128), jnp.bfloat16),
            dma((5,)),
            dma,
            dma,
            dma((2, 7)),
            dma((16,)),
            dma((2, 3)),
            dma((8,)),
            dma((BANDS - 1,)),
            dma((BANDS,)),
        ],
        compiler_params=pltpu.CompilerParams(
            vmem_limit_bytes=60 << 20, collective_id=0, has_side_effects=True
        ),
    )(adjoint_tend[0, :, 0, :], trajectory[:, 0, :], coupling, row_lat, row_points, wave_order)
    return spectra.transpose(0, 2, 1, 3)[None]


def solution(mesh):
    return jax.shard_map(
        body,
        mesh=mesh,
        in_specs=(
            P("col", None, "band", None),
            P(None, "band", "col"),
            P(),
            P("band"),
            P("band"),
            P(),
        ),
        out_specs=P("col", None, None, None, "band"),
        check_vma=False,
    )
```

```python
import jax
import jax.numpy as jnp
from jax import lax
from jax.experimental import pallas as pl
from jax.experimental.pallas import tpu as pltpu
from jax.sharding import PartitionSpec as P

LEVELS = 8
LATITUDES = 2560
VARS = 40
POINTS = 5120
WAVES = 768
PIECE = 80
BANDS = 12
OWN_WAVES = 64
LANES = 2 * BANDS * OWN_WAVES
STEP = 2 * PIECE
SINE = (6.283185005187988, -41.34165573120117, 81.60100555419922, -76.5497817993164, 39.536705017089844)
MESH = pl.DeviceIdType.MESH
NEAR_FIRST = (1, 7, 2, 6, 3, 5, 4)


def sine_turns(v):
    u = v * v
    p = jnp.full_like(u, SINE[-1])
    for c in SINE[-2::-1]:
        p = p * u + c
    return p * v


def cosine_turns(t):
    v = 0.25 - jnp.abs(t)
    return sine_turns(jnp.maximum(v, -0.5 - v))


def turns(pm, n, rn):
    q = jnp.floor(pm * rn + 0.5)
    return (pm - q * n) * rn


def tables(points, waves_ref, fine_ref, a_ref, b_ref, chosen):
    lane = lax.broadcasted_iota(jnp.int32, (8, 128), 1)
    first_half = lane < 64
    n8 = jnp.full((8, 128), points.astype(jnp.float32), jnp.float32)
    rn8 = 1.0 / n8
    root8 = 1.0 / jnp.sqrt(n8)
    shift8 = jnp.where(first_half, 0.0, 0.25)
    sign8 = jnp.where(first_half, 1.0, -1.0)
    row8 = lax.broadcasted_iota(jnp.int32, (8, 128), 0).astype(jnp.float32)
    for tile in chosen:
        pair = jnp.broadcast_to(waves_ref[pl.ds(128 * tile, 128)].reshape(1, 128), (8, 128)).astype(jnp.float32)
        turned = pltpu.roll(pair, 64, 1)
        for odd in range(2):
            w8 = jnp.where(first_half, pair, turned) if odd == 0 else jnp.where(first_half, turned, pair)
            at = (2 * tile + odd) * 128
            scale = jnp.where(2.0 * w8 < n8, root8, 0.0)
            for k in range(4):
                t = turns((row8 + 8.0 * k) * STEP * w8, n8, rn8)
                a_ref[8 * k : 8 * k + 8, at : at + 128] = scale * sign8 * cosine_turns(t)
                b_ref[8 * k : 8 * k + 8, at : at + 128] = -scale * cosine_turns(t - 0.25)
            wide = lambda v: jnp.broadcast_to(v[None], (PIECE // 8, 8, 128)).reshape(PIECE, 128)
            for zz in range(2):
                p0 = lax.broadcasted_iota(jnp.int32, (PIECE, 128), 0).astype(jnp.float32) + float(PIECE * zz)
                t = turns(p0 * wide(w8), wide(n8), wide(rn8))
                fine_ref[zz, 0:PIECE, at : at + 128] = cosine_turns(t - wide(shift8)).astype(jnp.bfloat16)


def repack(tend_ref, block_ref, xp):
    lane = lax.broadcasted_iota(jnp.int32, (VARS, 128), 1)
    for zz in range(2):
        for y in range(8):
            tile, at = divmod(STEP * y + PIECE * zz, 128)

            def load(k):
                start = pl.multiple_of(xp * 1280 + 128 * k, 128)
                return pltpu.roll(tend_ref[:, pl.ds(start, 128)].astype(jnp.float32), (128 - at) % 128, 1)

            piece = load(tile)
            if at + PIECE > 128:
                piece = jnp.where(lane < 128 - at, piece, load(tile + 1))
            block_ref[2 * xp + zz, :, 128 * y : 128 * y + 128] = piece


def column(turning, points, block_ref, piece_ref, coup_ref, back_ref, x_ref, xp, zz):
    zeros = jnp.zeros((VARS, 128 - PIECE), jnp.float32)
    pieces = [piece_ref[16 * xp + 2 * y + zz].astype(jnp.float32) for y in range(8)]
    traj = jnp.concatenate([part for piece in pieces for part in (piece, zeros)], axis=1)
    tend = block_ref[2 * xp + zz]
    driven = jnp.dot(coup_ref[...], traj.astype(jnp.bfloat16), preferred_element_type=jnp.float32)
    weighted = tend * (1.0 + traj)
    high = weighted.astype(jnp.bfloat16).astype(jnp.float32)
    both = jnp.concatenate([high, weighted - high], axis=0).astype(jnp.bfloat16)
    backed = jnp.dot(back_ref[...], both, preferred_element_type=jnp.float32)
    total = backed + tend * driven
    turn = jnp.tile(turning, (1, 8))
    total = jnp.concatenate(
        [
            total[:LEVELS] - turn * tend[LEVELS : 2 * LEVELS],
            total[LEVELS : 2 * LEVELS] + turn * tend[:LEVELS],
            total[2 * LEVELS :],
        ],
        axis=0,
    )
    q = lax.broadcasted_iota(jnp.int32, (VARS, 128), 1)
    first = xp * 1280 + zz * PIECE
    rows = []
    for y in range(8):
        keep = (q < PIECE) & (q + (first + STEP * y) < points)
        rows.append(jnp.where(keep, total[:, 128 * y : 128 * y + 128], 0.0))
    x_ref[...] = jnp.concatenate(rows, axis=0).astype(jnp.bfloat16)


def transform(x_ref, fine_ref, a_ref, b_ref, xp, zz, j):
    at = pl.multiple_of(j * 256, 256)
    y = jnp.dot(x_ref[...], fine_ref[zz, :, pl.ds(at, 256)], preferred_element_type=jnp.float32)
    a = a_ref[pl.ds(pl.multiple_of(8 * xp, 8), 8), pl.ds(at, 256)]
    b = b_ref[pl.ds(pl.multiple_of(8 * xp, 8), 8), pl.ds(at, 256)]
    u = y[:VARS] * a[0:1]
    v = y[:VARS] * b[0:1]
    for k in range(1, 8):
        part = y[VARS * k : VARS * (k + 1)]
        u = u + part * a[k : k + 1]
        v = v + part * b[k : k + 1]
    return u, v


def kernel(
    lat_ref, tend_hbm, traj_hbm, coup_hbm, waves_hbm, out_hbm,
    coup_ref, back_ref, waves_ref, tend_ref, block_ref, piece_ref,
    fine_ref, a_ref, b_ref, x_ref, u_ref, v_ref, send_ref,
    load_sem, own_sem, piece_recv, z_send, y_send, x_send, band_send, band_recv,
):
    band = lax.axis_index("band")
    col = lax.axis_index("col")
    x, y, z = col // 16, (col // 2) % 8, col % 2
    mate = col + 1 - 2 * z
    z_peer = (band, mate)
    y_peers = {s: (band, 16 * x + 2 * ((y + s) % 8) + z) for s in NEAR_FIRST}
    x_peers = [(band, 16 * ((x + s) % 4) + 2 * y + z) for s in (1, 3, 2)]
    band_peers = [((band + s) % BANDS, col) for s in range(1, BANDS)]

    loads = [
        pltpu.make_async_copy(source, target, load_sem.at[i])
        for i, (source, target) in enumerate(
            [(waves_hbm, waves_ref), (coup_hbm, coup_ref), (tend_hbm, tend_ref)]
        )
    ]
    for load in loads:
        load.start()
    keep = pltpu.make_async_copy(traj_hbm, piece_ref.at[col], own_sem)
    keep.start()
    barrier = pltpu.get_barrier_semaphore()
    peers = [z_peer] + list(y_peers.values()) + x_peers + band_peers
    for peer in peers:
        pl.semaphore_signal(barrier, inc=1, device_id=peer, device_id_type=MESH)
    pl.semaphore_wait(barrier, len(peers))

    sent = []

    def send(source, slot, send_sem, peer):
        copy = pltpu.make_async_remote_copy(
            src_ref=source,
            dst_ref=piece_ref.at[slot],
            send_sem=send_sem,
            recv_sem=piece_recv.at[slot],
            device_id=peer,
            device_id_type=MESH,
        )
        copy.start()
        sent.append(copy)

    def arrive(slot):
        pltpu.make_async_remote_copy(
            src_ref=piece_ref.at[slot],
            dst_ref=piece_ref.at[slot],
            send_sem=z_send,
            recv_sem=piece_recv.at[slot],
            device_id=z_peer,
            device_id_type=MESH,
        ).wait_recv()

    def along(source, slot, own):
        for s in NEAR_FIRST:
            send(source, slot, y_send.at[own, s], y_peers[s])

    def across(source, slot, own, s):
        for k, peer in enumerate(x_peers):
            send(source, slot, x_send.at[own, s, k], peer)

    send(traj_hbm, col, z_send, z_peer)
    along(traj_hbm, col, 0)
    across(traj_hbm, col, 0, 0)

    def pass_on(zz, own, offsets):
        for s in offsets:
            slot = 16 * x + 2 * ((y + s) % 8) + zz
            arrive(slot)
            across(piece_ref.at[slot], slot, own, s)

    loads[0].wait()
    latitude = lat_ref[0]
    points = jnp.minimum(20 + 4 * jnp.minimum(latitude, LATITUDES - 1 - latitude), POINTS)
    tables(points, waves_ref, fine_ref, a_ref, b_ref, range(3))
    pass_on(z, 0, NEAR_FIRST[:2])
    tables(points, waves_ref, fine_ref, a_ref, b_ref, range(3, 6))
    pass_on(z, 0, NEAR_FIRST[2:4])
    for load in loads[1:]:
        load.wait()
    ratio = (2.0 * jnp.full((8, 128), latitude.astype(jnp.float32)) + 1.0) / LATITUDES
    turning = sine_turns(0.25 - 0.25 * ratio)
    back = coup_ref[...].astype(jnp.float32).T.astype(jnp.bfloat16)
    back_ref[...] = jnp.concatenate([back, back], axis=1)
    for zz in range(2):
        fine_ref[zz, PIECE:] = jnp.zeros((128 - PIECE, LANES), jnp.bfloat16)
    pass_on(z, 0, NEAR_FIRST[4:])
    arrive(mate)
    along(piece_ref.at[mate], mate, 1)
    across(piece_ref.at[mate], mate, 1, 0)

    def two(xp, carry):
        repack(tend_ref, block_ref, xp)
        return carry

    lax.fori_loop(0, 4, two, 0)
    keep.wait()

    def add(xp, zz, first):
        column(turning, points, block_ref, piece_ref, coup_ref, back_ref, x_ref, xp, zz)

        def tile(j, carry):
            u, v = transform(x_ref, fine_ref, a_ref, b_ref, xp, zz, j)
            if not first:
                u = u + u_ref[j]
                v = v + v_ref[j]
            u_ref[j] = u
            v_ref[j] = v
            return carry

        lax.fori_loop(0, 6, tile, 0, unroll=True)

    def take(xp, zz):
        for k in range(8):
            arrive(16 * xp + 2 * k + zz)

    pass_on(1 - z, 1, NEAR_FIRST[:2])
    add(x, z, True)
    pass_on(1 - z, 1, NEAR_FIRST[2:])
    for s in (1, 3, 2):
        take((x + s) % 4, z)
        add((x + s) % 4, z, False)
    add(x, 1 - z, False)
    for s in (1, 3):
        take((x + s) % 4, 1 - z)
        add((x + s) % 4, 1 - z, False)

    xp, zz = (x + 2) % 4, 1 - z
    take(xp, zz)
    column(turning, points, block_ref, piece_ref, coup_ref, back_ref, x_ref, xp, zz)
    own = pltpu.make_async_copy(send_ref.at[band], out_hbm.at[band], own_sem)

    def to_band(d):
        return pltpu.make_async_remote_copy(
            src_ref=send_ref.at[d],
            dst_ref=out_hbm.at[band],
            send_sem=band_send.at[d],
            recv_sem=band_recv.at[band],
            device_id=(d, col),
            device_id_type=MESH,
        )

    def last(s, carry):
        j = jnp.where(band >= BANDS // 2, s, BANDS // 2 - 1 - s)
        u, v = transform(x_ref, fine_ref, a_ref, b_ref, xp, zz, j)
        u = u + u_ref[j]
        v = v + v_ref[j]
        for odd in range(2):
            d = 2 * j + odd
            half = slice(128 * odd, 128 * odd + 128)
            send_ref[d] = (u[:, half] + pltpu.roll(v[:, half], 64, 1)).astype(jnp.bfloat16)

            @pl.when(d != band)
            def _():
                to_band(d).start()

        return carry

    lax.fori_loop(0, 6, last, 0, unroll=True)
    own.start()
    for s in range(1, BANDS):
        source = (band + s) % BANDS
        pltpu.make_async_remote_copy(
            src_ref=send_ref.at[source],
            dst_ref=out_hbm.at[source],
            send_sem=band_send.at[source],
            recv_sem=band_recv.at[source],
            device_id=band_peers[0],
            device_id_type=MESH,
        ).wait_recv()
    own.wait()
    for copy in sent:
        copy.wait_send()
    for s in range(1, BANDS):
        to_band((band + s) % BANDS).wait_send()


def body(adjoint_tend, trajectory, coupling, row_lat, row_points, wave_order):
    vmem, smem, dma = pltpu.VMEM, pltpu.SMEM, pltpu.SemaphoreType.DMA
    arrays = [
        pltpu.with_memory_space_constraint(array, pltpu.HBM)
        for array in (adjoint_tend[0, :, 0, :], trajectory[:, 0, :], coupling, wave_order)
    ]
    parts = pl.pallas_call(
        kernel,
        out_shape=jax.ShapeDtypeStruct((BANDS, VARS, 128), jnp.bfloat16),
        in_specs=[pl.BlockSpec(memory_space=smem)] + [pl.BlockSpec(memory_space=pltpu.HBM)] * 4,
        out_specs=pl.BlockSpec(memory_space=vmem),
        scratch_shapes=[
            vmem((VARS, VARS), jnp.bfloat16),
            vmem((VARS, 2 * VARS), jnp.bfloat16),
            vmem((WAVES,), jnp.int32),
            vmem((VARS, POINTS), jnp.bfloat16),
            vmem((8, VARS, 1024), jnp.float32),
            vmem((64, VARS, PIECE), jnp.bfloat16),
            vmem((2, 128, LANES), jnp.bfloat16),
            vmem((32, LANES), jnp.float32),
            vmem((32, LANES), jnp.float32),
            vmem((8 * VARS, 128), jnp.bfloat16),
            vmem((6, VARS, 256), jnp.float32),
            vmem((6, VARS, 256), jnp.float32),
            vmem((BANDS, VARS, 128), jnp.bfloat16),
            dma((3,)),
            dma,
            dma((64,)),
            dma,
            dma((2, 8)),
            dma((2, 8, 3)),
            dma((BANDS,)),
            dma((BANDS,)),
        ],
        compiler_params=pltpu.CompilerParams(
            vmem_limit_bytes=32 << 20, collective_id=0, has_side_effects=True
        ),
    )(row_lat, *arrays)
    spectra = jnp.stack([parts[:, :, :OWN_WAVES], parts[:, :, OWN_WAVES:]])
    return spectra.transpose(0, 2, 1, 3)[None]


def solution(mesh):
    return jax.shard_map(
        body,
        mesh=mesh,
        in_specs=(
            P("col", None, "band", None),
            P(None, "band", "col"),
            P(),
            P("band"),
            P("band"),
            P(),
        ),
        out_specs=P("col", None, None, None, "band"),
        check_vma=False,
    )
```

```python
import jax
import jax.numpy as jnp
from jax import lax
from jax.experimental import pallas as pl
from jax.experimental.pallas import tpu as pltpu
from jax.sharding import PartitionSpec as P

LEVELS = 8
LATITUDES = 2560
VARS = 40
POINTS = 5120
WAVES = 768
PIECE = 80
BANDS = 12
OWN_WAVES = 64
LANES = 2 * BANDS * OWN_WAVES
STEP = 2 * PIECE
SINE = (6.283185005187988, -41.34165573120117, 81.60100555419922, -76.5497817993164, 39.536705017089844)
MESH = pl.DeviceIdType.MESH
NEAR_FIRST = (1, 7, 2, 6, 3, 5, 4)


def sine_turns(v):
    u = v * v
    p = jnp.full_like(u, SINE[-1])
    for c in SINE[-2::-1]:
        p = p * u + c
    return p * v


def cosine_turns(t):
    v = 0.25 - jnp.abs(t)
    return sine_turns(jnp.maximum(v, -0.5 - v))


def turns(pm, n, rn):
    q = jnp.floor(pm * rn + 0.5)
    return (pm - q * n) * rn


def tables(points, waves_ref, fine_ref, a_ref, b_ref, chosen):
    lane = lax.broadcasted_iota(jnp.int32, (8, 128), 1)
    first_half = lane < 64
    n8 = jnp.full((8, 128), points.astype(jnp.float32), jnp.float32)
    rn8 = 1.0 / n8
    root8 = 1.0 / jnp.sqrt(n8)
    shift8 = jnp.where(first_half, 0.0, 0.25)
    sign8 = jnp.where(first_half, 1.0, -1.0)
    row8 = lax.broadcasted_iota(jnp.int32, (8, 128), 0).astype(jnp.float32)
    for tile in chosen:
        pair = jnp.broadcast_to(waves_ref[pl.ds(128 * tile, 128)].reshape(1, 128), (8, 128)).astype(jnp.float32)
        turned = pltpu.roll(pair, 64, 1)
        for odd in range(2):
            w8 = jnp.where(first_half, pair, turned) if odd == 0 else jnp.where(first_half, turned, pair)
            at = (2 * tile + odd) * 128
            scale = jnp.where(2.0 * w8 < n8, root8, 0.0)
            for k in range(4):
                t = turns((row8 + 8.0 * k) * STEP * w8, n8, rn8)
                a_ref[8 * k : 8 * k + 8, at : at + 128] = scale * sign8 * cosine_turns(t)
                b_ref[8 * k : 8 * k + 8, at : at + 128] = -scale * cosine_turns(t - 0.25)
            wide = lambda v: jnp.broadcast_to(v[None], (PIECE // 8, 8, 128)).reshape(PIECE, 128)
            for zz in range(2):
                p0 = lax.broadcasted_iota(jnp.int32, (PIECE, 128), 0).astype(jnp.float32) + float(PIECE * zz)
                t = turns(p0 * wide(w8), wide(n8), wide(rn8))
                fine_ref[zz, 0:PIECE, at : at + 128] = cosine_turns(t - wide(shift8)).astype(jnp.bfloat16)


def repack(tend_ref, block_ref, xp):
    lane = lax.broadcasted_iota(jnp.int32, (VARS, 128), 1)
    for zz in range(2):
        for y in range(8):
            tile, at = divmod(STEP * y + PIECE * zz, 128)

            def load(k):
                start = pl.multiple_of(xp * 1280 + 128 * k, 128)
                return pltpu.roll(tend_ref[:, pl.ds(start, 128)].astype(jnp.float32), (128 - at) % 128, 1)

            piece = load(tile)
            if at + PIECE > 128:
                piece = jnp.where(lane < 128 - at, piece, load(tile + 1))
            block_ref[2 * xp + zz, :, 128 * y : 128 * y + 128] = piece


def column(turning, points, block_ref, piece_ref, coup_ref, back_ref, x_ref, xp, zz):
    zeros = jnp.zeros((VARS, 128 - PIECE), jnp.float32)
    pieces = [piece_ref[16 * xp + 2 * y + zz].astype(jnp.float32) for y in range(8)]
    traj = jnp.concatenate([part for piece in pieces for part in (piece, zeros)], axis=1)
    tend = block_ref[2 * xp + zz]
    driven = jnp.dot(coup_ref[...], traj.astype(jnp.bfloat16), preferred_element_type=jnp.float32)
    weighted = tend * (1.0 + traj)
    high = weighted.astype(jnp.bfloat16).astype(jnp.float32)
    both = jnp.concatenate([high, weighted - high], axis=0).astype(jnp.bfloat16)
    backed = jnp.dot(back_ref[...], both, preferred_element_type=jnp.float32)
    total = backed + tend * driven
    turn = jnp.tile(turning, (1, 8))
    total = jnp.concatenate(
        [
            total[:LEVELS] - turn * tend[LEVELS : 2 * LEVELS],
            total[LEVELS : 2 * LEVELS] + turn * tend[:LEVELS],
            total[2 * LEVELS :],
        ],
        axis=0,
    )
    q = lax.broadcasted_iota(jnp.int32, (VARS, 128), 1)
    first = xp * 1280 + zz * PIECE
    rows = []
    for y in range(8):
        keep = (q < PIECE) & (q + (first + STEP * y) < points)
        rows.append(jnp.where(keep, total[:, 128 * y : 128 * y + 128], 0.0))
    x_ref[...] = jnp.concatenate(rows, axis=0).astype(jnp.bfloat16)


def transform(x_ref, fine_ref, a_ref, b_ref, xp, zz, j):
    at = pl.multiple_of(j * 256, 256)
    y = jnp.dot(x_ref[...], fine_ref[zz, :, pl.ds(at, 256)], preferred_element_type=jnp.float32)
    a = a_ref[pl.ds(pl.multiple_of(8 * xp, 8), 8), pl.ds(at, 256)]
    b = b_ref[pl.ds(pl.multiple_of(8 * xp, 8), 8), pl.ds(at, 256)]
    u = y[:VARS] * a[0:1]
    v = y[:VARS] * b[0:1]
    for k in range(1, 8):
        part = y[VARS * k : VARS * (k + 1)]
        u = u + part * a[k : k + 1]
        v = v + part * b[k : k + 1]
    return u, v


def kernel(
    lat_ref, tend_hbm, traj_hbm, coup_hbm, waves_hbm, out_hbm,
    coup_ref, back_ref, waves_ref, tend_ref, block_ref, piece_ref,
    fine_ref, a_ref, b_ref, x_ref, u_ref, v_ref, send_ref,
    load_sem, own_sem, piece_recv, z_send, y_send, x_send, band_send, band_recv, known,
):
    band = lax.axis_index("band")
    col = lax.axis_index("col")
    x, y, z = col // 16, (col // 2) % 8, col % 2
    mate = col + 1 - 2 * z
    z_peer = (band, mate)
    y_peers = {s: (band, 16 * x + 2 * ((y + s) % 8) + z) for s in NEAR_FIRST}
    x_peers = [(band, 16 * ((x + s) % 4) + 2 * y + z) for s in (1, 3, 2)]
    band_peers = [((band + s) % BANDS, col) for s in range(1, BANDS)]

    loads = [
        pltpu.make_async_copy(source, target, load_sem.at[i])
        for i, (source, target) in enumerate(
            [(waves_hbm, waves_ref), (coup_hbm, coup_ref), (tend_hbm, tend_ref)]
        )
    ]
    for load in loads:
        load.start()
    keep = pltpu.make_async_copy(traj_hbm, piece_ref.at[col], own_sem)
    keep.start()
    barrier = pltpu.get_barrier_semaphore()
    level = band // 2

    def near(step, act):
        for sign in (-1, 1):

            @pl.when((level + sign * step >= 0) & (level + sign * step < BANDS // 2))
            def _():
                act((band + 2 * sign * step, col))

    def beside(step):
        return jnp.where(level >= step, 1, 0) + jnp.where(level < BANDS // 2 - step, 1, 0)

    def call(semaphore, peer):
        pl.semaphore_signal(semaphore, inc=1, device_id=peer, device_id_type=MESH)

    core_peer = (band + 1 - 2 * (band % 2), col)
    @pl.when(z == 0)
    def _():
        call(barrier, z_peer)

    for peer in list(y_peers.values()) + x_peers + [core_peer]:
        call(barrier, peer)
    near(1, lambda peer: call(barrier, peer))
    pl.semaphore_wait(barrier, 11 + beside(1) + z)

    sent = []

    def send(source, slot, send_sem, peer):
        copy = pltpu.make_async_remote_copy(
            src_ref=source,
            dst_ref=piece_ref.at[slot],
            send_sem=send_sem,
            recv_sem=piece_recv.at[slot],
            device_id=peer,
            device_id_type=MESH,
        )
        copy.start()
        sent.append(copy)

    def arrive(slot):
        pltpu.make_async_remote_copy(
            src_ref=piece_ref.at[slot],
            dst_ref=piece_ref.at[slot],
            send_sem=z_send,
            recv_sem=piece_recv.at[slot],
            device_id=z_peer,
            device_id_type=MESH,
        ).wait_recv()

    def along(source, slot, own):
        for s in NEAR_FIRST:
            send(source, slot, y_send.at[own, s], y_peers[s])

    def across(source, slot, own, s):
        for k, peer in enumerate(x_peers):
            send(source, slot, x_send.at[own, s, k], peer)

    exchange = pltpu.make_async_remote_copy(
        src_ref=traj_hbm,
        dst_ref=piece_ref.at[col],
        send_sem=z_send,
        recv_sem=piece_recv.at[col],
        device_id=z_peer,
        device_id_type=MESH,
    )
    sent.append(exchange)

    @pl.when(z == 1)
    def _():
        exchange.start()

    along(traj_hbm, col, 0)
    across(traj_hbm, col, 0, 0)
    near(1, lambda peer: call(known.at[0], peer))

    def pass_on(zz, own, offsets):
        for s in offsets:
            slot = 16 * x + 2 * ((y + s) % 8) + zz
            arrive(slot)
            across(piece_ref.at[slot], slot, own, s)

    loads[0].wait()
    latitude = lat_ref[0]
    points = jnp.minimum(20 + 4 * jnp.minimum(latitude, LATITUDES - 1 - latitude), POINTS)
    tables(points, waves_ref, fine_ref, a_ref, b_ref, range(3))
    pass_on(z, 0, NEAR_FIRST[:2])
    pl.semaphore_wait(known.at[0], beside(1))
    near(2, lambda peer: call(known.at[1], peer))
    tables(points, waves_ref, fine_ref, a_ref, b_ref, range(3, 6))
    pass_on(z, 0, NEAR_FIRST[2:4])
    for load in loads[1:]:
        load.wait()
    ratio = (2.0 * jnp.full((8, 128), latitude.astype(jnp.float32)) + 1.0) / LATITUDES
    turning = sine_turns(0.25 - 0.25 * ratio)
    back = coup_ref[...].astype(jnp.float32).T.astype(jnp.bfloat16)
    back_ref[...] = jnp.concatenate([back, back], axis=1)
    for zz in range(2):
        fine_ref[zz, PIECE:] = jnp.zeros((128 - PIECE, LANES), jnp.bfloat16)
    pass_on(z, 0, NEAR_FIRST[4:])
    pl.semaphore_wait(known.at[1], beside(2))
    near(1, lambda peer: call(known.at[2], peer))
    arrive(mate)

    @pl.when(z == 0)
    def _():
        exchange.start()

    along(piece_ref.at[mate], mate, 1)
    across(piece_ref.at[mate], mate, 1, 0)

    def two(xp, carry):
        repack(tend_ref, block_ref, xp)
        return carry

    lax.fori_loop(0, 4, two, 0)
    pl.semaphore_wait(known.at[2], beside(1))
    call(known.at[3], core_peer)
    keep.wait()

    def add(xp, zz, first):
        column(turning, points, block_ref, piece_ref, coup_ref, back_ref, x_ref, xp, zz)

        def tile(j, carry):
            u, v = transform(x_ref, fine_ref, a_ref, b_ref, xp, zz, j)
            if not first:
                u = u + u_ref[j]
                v = v + v_ref[j]
            u_ref[j] = u
            v_ref[j] = v
            return carry

        lax.fori_loop(0, 6, tile, 0, unroll=True)

    def take(xp, zz):
        for k in range(8):
            arrive(16 * xp + 2 * k + zz)

    pass_on(1 - z, 1, NEAR_FIRST[:2])
    add(x, z, True)
    pass_on(1 - z, 1, NEAR_FIRST[2:])
    for s in (1, 3, 2):
        take((x + s) % 4, z)
        add((x + s) % 4, z, False)
    add(x, 1 - z, False)
    for s in (1, 3):
        take((x + s) % 4, 1 - z)
        add((x + s) % 4, 1 - z, False)

    pl.semaphore_wait(known.at[3], 1)
    xp, zz = (x + 2) % 4, 1 - z
    take(xp, zz)
    column(turning, points, block_ref, piece_ref, coup_ref, back_ref, x_ref, xp, zz)
    own = pltpu.make_async_copy(send_ref.at[band], out_hbm.at[band], own_sem)

    def to_band(d):
        return pltpu.make_async_remote_copy(
            src_ref=send_ref.at[d],
            dst_ref=out_hbm.at[band],
            send_sem=band_send.at[d],
            recv_sem=band_recv.at[band],
            device_id=(d, col),
            device_id_type=MESH,
        )

    def last(s, carry):
        j = jnp.where(band >= BANDS // 2, s, BANDS // 2 - 1 - s)
        u, v = transform(x_ref, fine_ref, a_ref, b_ref, xp, zz, j)
        u = u + u_ref[j]
        v = v + v_ref[j]
        for odd in range(2):
            d = 2 * j + odd
            half = slice(128 * odd, 128 * odd + 128)
            send_ref[d] = (u[:, half] + pltpu.roll(v[:, half], 64, 1)).astype(jnp.bfloat16)

            @pl.when(d != band)
            def _():
                to_band(d).start()

        return carry

    lax.fori_loop(0, 6, last, 0, unroll=True)
    own.start()
    for s in range(1, BANDS):
        source = (band + s) % BANDS
        pltpu.make_async_remote_copy(
            src_ref=send_ref.at[source],
            dst_ref=out_hbm.at[source],
            send_sem=band_send.at[source],
            recv_sem=band_recv.at[source],
            device_id=band_peers[0],
            device_id_type=MESH,
        ).wait_recv()
    own.wait()
    for copy in sent:
        copy.wait_send()
    for s in range(1, BANDS):
        to_band((band + s) % BANDS).wait_send()


def body(adjoint_tend, trajectory, coupling, row_lat, row_points, wave_order):
    vmem, smem, dma = pltpu.VMEM, pltpu.SMEM, pltpu.SemaphoreType.DMA
    arrays = [
        pltpu.with_memory_space_constraint(array, pltpu.HBM)
        for array in (adjoint_tend[0, :, 0, :], trajectory[:, 0, :], coupling, wave_order)
    ]
    parts = pl.pallas_call(
        kernel,
        out_shape=jax.ShapeDtypeStruct((BANDS, VARS, 128), jnp.bfloat16),
        in_specs=[pl.BlockSpec(memory_space=smem)] + [pl.BlockSpec(memory_space=pltpu.HBM)] * 4,
        out_specs=pl.BlockSpec(memory_space=vmem),
        scratch_shapes=[
            vmem((VARS, VARS), jnp.bfloat16),
            vmem((VARS, 2 * VARS), jnp.bfloat16),
            vmem((WAVES,), jnp.int32),
            vmem((VARS, POINTS), jnp.bfloat16),
            vmem((8, VARS, 1024), jnp.float32),
            vmem((64, VARS, PIECE), jnp.bfloat16),
            vmem((2, 128, LANES), jnp.bfloat16),
            vmem((32, LANES), jnp.float32),
            vmem((32, LANES), jnp.float32),
            vmem((8 * VARS, 128), jnp.bfloat16),
            vmem((6, VARS, 256), jnp.float32),
            vmem((6, VARS, 256), jnp.float32),
            vmem((BANDS, VARS, 128), jnp.bfloat16),
            dma((3,)),
            dma,
            dma((64,)),
            dma,
            dma((2, 8)),
            dma((2, 8, 3)),
            dma((BANDS,)),
            dma((BANDS,)),
            pltpu.SemaphoreType.REGULAR((4,)),
        ],
        compiler_params=pltpu.CompilerParams(
            vmem_limit_bytes=32 << 20, collective_id=0, has_side_effects=True
        ),
    )(row_lat, *arrays)
    spectra = jnp.stack([parts[:, :, :OWN_WAVES], parts[:, :, OWN_WAVES:]])
    return spectra.transpose(0, 2, 1, 3)[None]


def solution(mesh):
    return jax.shard_map(
        body,
        mesh=mesh,
        in_specs=(
            P("col", None, "band", None),
            P(None, "band", "col"),
            P(),
            P("band"),
            P("band"),
            P(),
        ),
        out_specs=P("col", None, None, None, "band"),
        check_vma=False,
    )
```

```python
import jax
import jax.numpy as jnp
from jax import lax
from jax.experimental import pallas as pl
from jax.experimental.pallas import tpu as pltpu
from jax.sharding import PartitionSpec as P

LEVELS = 8
LATITUDES = 2560
VARS = 40
POINTS = 5120
WAVES = 768
PIECE = 80
BANDS = 12
OWN_WAVES = 64
LANES = 2 * BANDS * OWN_WAVES
STEP = 2 * PIECE
SINE = (6.283185005187988, -41.34165573120117, 81.60100555419922, -76.5497817993164, 39.536705017089844)
MESH = pl.DeviceIdType.MESH
NEAR_FIRST = (1, 7, 2, 6, 3, 5, 4)


def sine_turns(v):
    u = v * v
    p = jnp.full_like(u, SINE[-1])
    for c in SINE[-2::-1]:
        p = p * u + c
    return p * v


def cosine_turns(t):
    v = 0.25 - jnp.abs(t)
    return sine_turns(jnp.maximum(v, -0.5 - v))


def turns(pm, n, rn):
    q = jnp.floor(pm * rn + 0.5)
    return (pm - q * n) * rn


def tables(points, waves_ref, fine_ref, a_ref, b_ref, chosen):
    lane = lax.broadcasted_iota(jnp.int32, (8, 128), 1)
    first_half = lane < 64
    n8 = jnp.full((8, 128), points.astype(jnp.float32), jnp.float32)
    rn8 = 1.0 / n8
    root8 = 1.0 / jnp.sqrt(n8)
    shift8 = jnp.where(first_half, 0.0, 0.25)
    sign8 = jnp.where(first_half, 1.0, -1.0)
    row8 = lax.broadcasted_iota(jnp.int32, (8, 128), 0).astype(jnp.float32)
    for tile in chosen:
        pair = jnp.broadcast_to(waves_ref[pl.ds(128 * tile, 128)].reshape(1, 128), (8, 128)).astype(jnp.float32)
        turned = pltpu.roll(pair, 64, 1)
        for odd in range(2):
            w8 = jnp.where(first_half, pair, turned) if odd == 0 else jnp.where(first_half, turned, pair)
            at = (2 * tile + odd) * 128
            scale = jnp.where(2.0 * w8 < n8, root8, 0.0)
            for k in range(4):
                t = turns((row8 + 8.0 * k) * STEP * w8, n8, rn8)
                a_ref[8 * k : 8 * k + 8, at : at + 128] = scale * sign8 * cosine_turns(t)
                b_ref[8 * k : 8 * k + 8, at : at + 128] = -scale * cosine_turns(t - 0.25)
            wide = lambda v: jnp.broadcast_to(v[None], (PIECE // 8, 8, 128)).reshape(PIECE, 128)
            for zz in range(2):
                p0 = lax.broadcasted_iota(jnp.int32, (PIECE, 128), 0).astype(jnp.float32) + float(PIECE * zz)
                t = turns(p0 * wide(w8), wide(n8), wide(rn8))
                fine_ref[zz, 0:PIECE, at : at + 128] = cosine_turns(t - wide(shift8)).astype(jnp.bfloat16)


def repack(tend_ref, block_ref, xp):
    lane = lax.broadcasted_iota(jnp.int32, (VARS, 128), 1)
    for zz in range(2):
        for y in range(8):
            tile, at = divmod(STEP * y + PIECE * zz, 128)

            def load(k):
                start = pl.multiple_of(xp * 1280 + 128 * k, 128)
                return pltpu.roll(tend_ref[:, pl.ds(start, 128)].astype(jnp.float32), (128 - at) % 128, 1)

            piece = load(tile)
            if at + PIECE > 128:
                piece = jnp.where(lane < 128 - at, piece, load(tile + 1))
            block_ref[2 * xp + zz, :, 128 * y : 128 * y + 128] = piece


def column(turning, points, block_ref, piece_ref, coup_ref, back_ref, x_ref, xp, zz):
    zeros = jnp.zeros((VARS, 128 - PIECE), jnp.float32)
    pieces = [piece_ref[16 * xp + 2 * y + zz].astype(jnp.float32) for y in range(8)]
    traj = jnp.concatenate([part for piece in pieces for part in (piece, zeros)], axis=1)
    tend = block_ref[2 * xp + zz]
    driven = jnp.dot(coup_ref[...], traj.astype(jnp.bfloat16), preferred_element_type=jnp.float32)
    weighted = tend * (1.0 + traj)
    high = weighted.astype(jnp.bfloat16).astype(jnp.float32)
    both = jnp.concatenate([high, weighted - high], axis=0).astype(jnp.bfloat16)
    backed = jnp.dot(back_ref[...], both, preferred_element_type=jnp.float32)
    total = backed + tend * driven
    turn = jnp.tile(turning, (1, 8))
    total = jnp.concatenate(
        [
            total[:LEVELS] - turn * tend[LEVELS : 2 * LEVELS],
            total[LEVELS : 2 * LEVELS] + turn * tend[:LEVELS],
            total[2 * LEVELS :],
        ],
        axis=0,
    )
    q = lax.broadcasted_iota(jnp.int32, (VARS, 128), 1)
    first = xp * 1280 + zz * PIECE
    rows = []
    for y in range(8):
        keep = (q < PIECE) & (q + (first + STEP * y) < points)
        rows.append(jnp.where(keep, total[:, 128 * y : 128 * y + 128], 0.0))
    x_ref[...] = jnp.concatenate(rows, axis=0).astype(jnp.bfloat16)


def transform(x_ref, fine_ref, a_ref, b_ref, xp, zz, j):
    at = pl.multiple_of(j * 256, 256)
    y = jnp.dot(x_ref[...], fine_ref[zz, :, pl.ds(at, 256)], preferred_element_type=jnp.float32)
    a = a_ref[pl.ds(pl.multiple_of(8 * xp, 8), 8), pl.ds(at, 256)]
    b = b_ref[pl.ds(pl.multiple_of(8 * xp, 8), 8), pl.ds(at, 256)]
    u = y[:VARS] * a[0:1]
    v = y[:VARS] * b[0:1]
    for k in range(1, 8):
        part = y[VARS * k : VARS * (k + 1)]
        u = u + part * a[k : k + 1]
        v = v + part * b[k : k + 1]
    return u, v


def kernel(
    lat_ref, tend_hbm, traj_hbm, coup_hbm, waves_hbm, out_ref,
    coup_ref, back_ref, waves_ref, tend_ref, block_ref, piece_ref,
    fine_ref, a_ref, b_ref, x_ref, u_ref, v_ref, send_ref, part_ref,
    load_sem, own_sem, piece_recv, z_send, y_send, x_send, band_send, band_recv, known,
):
    band = lax.axis_index("band")
    col = lax.axis_index("col")
    x, y, z = col // 16, (col // 2) % 8, col % 2
    mate = col + 1 - 2 * z
    z_peer = (band, mate)
    y_peers = {s: (band, 16 * x + 2 * ((y + s) % 8) + z) for s in NEAR_FIRST}
    x_peers = [(band, 16 * ((x + s) % 4) + 2 * y + z) for s in (1, 3, 2)]
    band_peers = [((band + s) % BANDS, col) for s in range(1, BANDS)]

    barrier = pltpu.get_barrier_semaphore()
    level = band // 2

    def near(step, act):
        for sign in (-1, 1):

            @pl.when((level + sign * step >= 0) & (level + sign * step < BANDS // 2))
            def _():
                act((band + 2 * sign * step, col))

    def beside(step):
        return jnp.where(level >= step, 1, 0) + jnp.where(level < BANDS // 2 - step, 1, 0)

    def call(semaphore, peer):
        pl.semaphore_signal(semaphore, inc=1, device_id=peer, device_id_type=MESH)

    core_peer = (band + 1 - 2 * (band % 2), col)
    @pl.when(z == 0)
    def _():
        call(barrier, z_peer)

    for peer in list(y_peers.values()) + x_peers + [core_peer]:
        call(barrier, peer)
    near(1, lambda peer: call(barrier, peer))
    loads = [
        pltpu.make_async_copy(source, target, load_sem.at[i])
        for i, (source, target) in enumerate(
            [(waves_hbm, waves_ref), (coup_hbm, coup_ref), (tend_hbm, tend_ref)]
        )
    ]
    for load in loads:
        load.start()
    keep = pltpu.make_async_copy(traj_hbm, piece_ref.at[col], own_sem)
    keep.start()
    pl.semaphore_wait(barrier, 11 + beside(1) + z)

    sent = []

    def send(source, slot, send_sem, peer):
        copy = pltpu.make_async_remote_copy(
            src_ref=source,
            dst_ref=piece_ref.at[slot],
            send_sem=send_sem,
            recv_sem=piece_recv.at[slot],
            device_id=peer,
            device_id_type=MESH,
        )
        copy.start()
        sent.append(copy)

    def arrive(slot):
        pltpu.make_async_remote_copy(
            src_ref=piece_ref.at[slot],
            dst_ref=piece_ref.at[slot],
            send_sem=z_send,
            recv_sem=piece_recv.at[slot],
            device_id=z_peer,
            device_id_type=MESH,
        ).wait_recv()

    def along(source, slot, own):
        for s in NEAR_FIRST:
            send(source, slot, y_send.at[own, s], y_peers[s])

    def across(source, slot, own, s):
        for k, peer in enumerate(x_peers):
            send(source, slot, x_send.at[own, s, k], peer)

    exchange = pltpu.make_async_remote_copy(
        src_ref=traj_hbm,
        dst_ref=piece_ref.at[col],
        send_sem=z_send,
        recv_sem=piece_recv.at[col],
        device_id=z_peer,
        device_id_type=MESH,
    )
    sent.append(exchange)

    @pl.when(z == 1)
    def _():
        exchange.start()

    along(traj_hbm, col, 0)
    across(traj_hbm, col, 0, 0)
    near(1, lambda peer: call(known.at[0], peer))

    def pass_on(zz, own, offsets):
        for s in offsets:
            slot = 16 * x + 2 * ((y + s) % 8) + zz
            arrive(slot)
            across(piece_ref.at[slot], slot, own, s)

    loads[0].wait()
    latitude = lat_ref[0]
    points = jnp.minimum(20 + 4 * jnp.minimum(latitude, LATITUDES - 1 - latitude), POINTS)
    tables(points, waves_ref, fine_ref, a_ref, b_ref, range(3))
    pass_on(z, 0, NEAR_FIRST[:2])
    pl.semaphore_wait(known.at[0], beside(1))
    near(2, lambda peer: call(known.at[1], peer))
    tables(points, waves_ref, fine_ref, a_ref, b_ref, range(3, 6))
    pass_on(z, 0, NEAR_FIRST[2:4])
    for load in loads[1:]:
        load.wait()
    ratio = (2.0 * jnp.full((8, 128), latitude.astype(jnp.float32)) + 1.0) / LATITUDES
    turning = sine_turns(0.25 - 0.25 * ratio)
    back = coup_ref[...].astype(jnp.float32).T.astype(jnp.bfloat16)
    back_ref[...] = jnp.concatenate([back, back], axis=1)
    for zz in range(2):
        fine_ref[zz, PIECE:] = jnp.zeros((128 - PIECE, LANES), jnp.bfloat16)

    def two(xp, carry):
        repack(tend_ref, block_ref, xp)
        return carry

    lax.fori_loop(0, 4, two, 0)
    keep.wait()

    def add(xp, zz, first):
        column(turning, points, block_ref, piece_ref, coup_ref, back_ref, x_ref, xp, zz)

        def tile(j, carry):
            u, v = transform(x_ref, fine_ref, a_ref, b_ref, xp, zz, j)
            if not first:
                u = u + u_ref[j]
                v = v + v_ref[j]
            u_ref[j] = u
            v_ref[j] = v
            return carry

        lax.fori_loop(0, 6, tile, 0, unroll=True)

    def take(xp, zz):
        for k in range(8):
            arrive(16 * xp + 2 * k + zz)

    pass_on(z, 0, NEAR_FIRST[4:])
    pl.semaphore_wait(known.at[1], beside(2))
    near(1, lambda peer: call(known.at[2], peer))
    add(x, z, True)
    arrive(mate)

    @pl.when(z == 0)
    def _():
        exchange.start()

    along(piece_ref.at[mate], mate, 1)
    across(piece_ref.at[mate], mate, 1, 0)

    take((x + 1) % 4, z)
    add((x + 1) % 4, z, False)
    take((x + 3) % 4, z)
    add((x + 3) % 4, z, False)
    take((x + 2) % 4, z)
    add((x + 2) % 4, z, False)
    pl.semaphore_wait(known.at[2], beside(1))
    call(known.at[3], core_peer)
    pass_on(1 - z, 1, NEAR_FIRST[:])
    add(x, 1 - z, False)
    for s in (1, 3):
        take((x + s) % 4, 1 - z)
        add((x + s) % 4, 1 - z, False)

    pl.semaphore_wait(known.at[3], 1)
    xp, zz = (x + 2) % 4, 1 - z
    take(xp, zz)
    column(turning, points, block_ref, piece_ref, coup_ref, back_ref, x_ref, xp, zz)

    def unpack(row, ref):
        both = ref[row].astype(jnp.float32)
        out_ref[0, row] = both[:, :OWN_WAVES].astype(jnp.bfloat16)
        out_ref[1, row] = both[:, OWN_WAVES:].astype(jnp.bfloat16)


    def to_band(d):
        return pltpu.make_async_remote_copy(
            src_ref=send_ref.at[d],
            dst_ref=part_ref.at[band],
            send_sem=band_send.at[d],
            recv_sem=band_recv.at[band],
            device_id=(d, col),
            device_id_type=MESH,
        )

    def last(s, carry):
        j = jnp.where(band >= BANDS // 2, s, BANDS // 2 - 1 - s)
        u, v = transform(x_ref, fine_ref, a_ref, b_ref, xp, zz, j)
        u = u + u_ref[j]
        v = v + v_ref[j]
        for odd in range(2):
            d = 2 * j + odd
            half = slice(128 * odd, 128 * odd + 128)
            send_ref[d] = (u[:, half] + pltpu.roll(v[:, half], 64, 1)).astype(jnp.bfloat16)

            @pl.when(d != band)
            def _():
                to_band(d).start()

        return carry

    lax.fori_loop(0, 6, last, 0, unroll=True)
    unpack(band, send_ref)
    for copy in sent:
        copy.wait_send()
    for s in range(1, BANDS):
        source = (band + s) % BANDS
        pltpu.make_async_remote_copy(
            src_ref=send_ref.at[source],
            dst_ref=part_ref.at[source],
            send_sem=band_send.at[source],
            recv_sem=band_recv.at[source],
            device_id=band_peers[0],
            device_id_type=MESH,
        ).wait_recv()
        unpack(source, part_ref)
    for s in range(1, BANDS):
        to_band((band + s) % BANDS).wait_send()


def body(adjoint_tend, trajectory, coupling, row_lat, row_points, wave_order):
    vmem, smem, dma = pltpu.VMEM, pltpu.SMEM, pltpu.SemaphoreType.DMA
    arrays = [
        pltpu.with_memory_space_constraint(array, pltpu.HBM)
        for array in (adjoint_tend[0, :, 0, :], trajectory[:, 0, :], coupling, wave_order)
    ]
    parts = pl.pallas_call(
        kernel,
        out_shape=jax.ShapeDtypeStruct((2, BANDS, VARS, OWN_WAVES), jnp.bfloat16),
        in_specs=[pl.BlockSpec(memory_space=smem)] + [pl.BlockSpec(memory_space=pltpu.HBM)] * 4,
        out_specs=pl.BlockSpec(memory_space=vmem),
        scratch_shapes=[
            vmem((VARS, VARS), jnp.bfloat16),
            vmem((VARS, 2 * VARS), jnp.bfloat16),
            vmem((WAVES,), jnp.int32),
            vmem((VARS, POINTS), jnp.bfloat16),
            vmem((8, VARS, 1024), jnp.float32),
            vmem((64, VARS, PIECE), jnp.bfloat16),
            vmem((2, 128, LANES), jnp.bfloat16),
            vmem((32, LANES), jnp.float32),
            vmem((32, LANES), jnp.float32),
            vmem((8 * VARS, 128), jnp.bfloat16),
            vmem((6, VARS, 256), jnp.float32),
            vmem((6, VARS, 256), jnp.float32),
            vmem((BANDS, VARS, 128), jnp.bfloat16),
            vmem((BANDS, VARS, 128), jnp.bfloat16),
            dma((3,)),
            dma,
            dma((64,)),
            dma,
            dma((2, 8)),
            dma((2, 8, 3)),
            dma((BANDS,)),
            dma((BANDS,)),
            pltpu.SemaphoreType.REGULAR((4,)),
        ],
        compiler_params=pltpu.CompilerParams(
            vmem_limit_bytes=32 << 20, collective_id=0, has_side_effects=True
        ),
    )(row_lat, *arrays)
    return parts.transpose(0, 2, 1, 3)[None]


def solution(mesh):
    return jax.shard_map(
        body,
        mesh=mesh,
        in_specs=(
            P("col", None, "band", None),
            P(None, "band", "col"),
            P(),
            P("band"),
            P("band"),
            P(),
        ),
        out_specs=P("col", None, None, None, "band"),
        check_vma=False,
    )
```

```python
import jax
import jax.numpy as jnp
from jax import lax
from jax.experimental import pallas as pl
from jax.experimental.pallas import tpu as pltpu
from jax.sharding import PartitionSpec as P

LEVELS = 8
LATITUDES = 2560
VARS = 40
POINTS = 5120
WAVES = 768
PIECE = 80
BANDS = 12
OWN_WAVES = 64
LANES = 2 * BANDS * OWN_WAVES
STEP = 2 * PIECE
SINE = (6.283185005187988, -41.34165573120117, 81.60100555419922, -76.5497817993164, 39.536705017089844)
MESH = pl.DeviceIdType.MESH
NEAR_FIRST = (1, 7, 2, 6, 3, 5, 4)


def sine_turns(v):
    u = v * v
    p = jnp.full_like(u, SINE[-1])
    for c in SINE[-2::-1]:
        p = p * u + c
    return p * v


def cosine_turns(t):
    v = 0.25 - jnp.abs(t)
    return sine_turns(jnp.maximum(v, -0.5 - v))


def turns(pm, n, rn):
    q = jnp.floor(pm * rn + 0.5)
    return (pm - q * n) * rn


def tables(points, waves_ref, fine_ref, a_ref, b_ref, chosen):
    lane = lax.broadcasted_iota(jnp.int32, (8, 128), 1)
    first_half = lane < 64
    n8 = jnp.full((8, 128), points.astype(jnp.float32), jnp.float32)
    rn8 = 1.0 / n8
    root8 = 1.0 / jnp.sqrt(n8)
    shift8 = jnp.where(first_half, 0.0, 0.25)
    sign8 = jnp.where(first_half, 1.0, -1.0)
    row8 = lax.broadcasted_iota(jnp.int32, (8, 128), 0).astype(jnp.float32)
    for tile in chosen:
        pair = jnp.broadcast_to(waves_ref[pl.ds(128 * tile, 128)].reshape(1, 128), (8, 128)).astype(jnp.float32)
        turned = pltpu.roll(pair, 64, 1)
        for odd in range(2):
            w8 = jnp.where(first_half, pair, turned) if odd == 0 else jnp.where(first_half, turned, pair)
            at = (2 * tile + odd) * 128
            scale = jnp.where(2.0 * w8 < n8, root8, 0.0)
            for k in range(4):
                t = turns((row8 + 8.0 * k) * STEP * w8, n8, rn8)
                a_ref[8 * k : 8 * k + 8, at : at + 128] = scale * sign8 * cosine_turns(t)
                b_ref[8 * k : 8 * k + 8, at : at + 128] = -scale * cosine_turns(t - 0.25)
            wide = lambda v: jnp.broadcast_to(v[None], (PIECE // 8, 8, 128)).reshape(PIECE, 128)
            for zz in range(2):
                p0 = lax.broadcasted_iota(jnp.int32, (PIECE, 128), 0).astype(jnp.float32) + float(PIECE * zz)
                t = turns(p0 * wide(w8), wide(n8), wide(rn8))
                fine_ref[zz, 0:PIECE, at : at + 128] = cosine_turns(t - wide(shift8)).astype(jnp.bfloat16)


def repack(tend_ref, block_ref, xp):
    lane = lax.broadcasted_iota(jnp.int32, (VARS, 128), 1)
    for zz in range(2):
        for y in range(8):
            tile, at = divmod(STEP * y + PIECE * zz, 128)

            def load(k):
                start = pl.multiple_of(xp * 1280 + 128 * k, 128)
                return pltpu.roll(tend_ref[:, pl.ds(start, 128)].astype(jnp.float32), (128 - at) % 128, 1)

            piece = load(tile)
            if at + PIECE > 128:
                piece = jnp.where(lane < 128 - at, piece, load(tile + 1))
            block_ref[2 * xp + zz, :, 128 * y : 128 * y + 128] = piece


def column(turning, points, block_ref, piece_ref, coup_ref, back_ref, x_ref, xp, zz):
    zeros = jnp.zeros((VARS, 128 - PIECE), jnp.float32)
    pieces = [piece_ref[16 * xp + 2 * y + zz].astype(jnp.float32) for y in range(8)]
    traj = jnp.concatenate([part for piece in pieces for part in (piece, zeros)], axis=1)
    tend = block_ref[2 * xp + zz]
    driven = jnp.dot(coup_ref[...], traj.astype(jnp.bfloat16), preferred_element_type=jnp.float32)
    weighted = tend * (1.0 + traj)
    high = weighted.astype(jnp.bfloat16).astype(jnp.float32)
    both = jnp.concatenate([high, weighted - high], axis=0).astype(jnp.bfloat16)
    backed = jnp.dot(back_ref[...], both, preferred_element_type=jnp.float32)
    total = backed + tend * driven
    turn = jnp.tile(turning, (1, 8))
    total = jnp.concatenate(
        [
            total[:LEVELS] - turn * tend[LEVELS : 2 * LEVELS],
            total[LEVELS : 2 * LEVELS] + turn * tend[:LEVELS],
            total[2 * LEVELS :],
        ],
        axis=0,
    )
    q = lax.broadcasted_iota(jnp.int32, (VARS, 128), 1)
    first = xp * 1280 + zz * PIECE
    rows = []
    for y in range(8):
        keep = (q < PIECE) & (q + (first + STEP * y) < points)
        rows.append(jnp.where(keep, total[:, 128 * y : 128 * y + 128], 0.0))
    x_ref[...] = jnp.concatenate(rows, axis=0).astype(jnp.bfloat16)


def transform(x_ref, fine_ref, a_ref, b_ref, xp, zz, j):
    at = pl.multiple_of(j * 256, 256)
    y = jnp.dot(x_ref[...], fine_ref[zz, :, pl.ds(at, 256)], preferred_element_type=jnp.float32)
    a = a_ref[pl.ds(pl.multiple_of(8 * xp, 8), 8), pl.ds(at, 256)]
    b = b_ref[pl.ds(pl.multiple_of(8 * xp, 8), 8), pl.ds(at, 256)]
    u = y[:VARS] * a[0:1]
    v = y[:VARS] * b[0:1]
    for k in range(1, 8):
        part = y[VARS * k : VARS * (k + 1)]
        u = u + part * a[k : k + 1]
        v = v + part * b[k : k + 1]
    return u, v


def kernel(
    lat_ref, tend_hbm, traj_hbm, coup_hbm, waves_hbm, out_ref,
    coup_ref, back_ref, waves_ref, tend_ref, block_ref, piece_ref,
    fine_ref, a_ref, b_ref, x_ref, u_ref, v_ref, send_ref, part_ref,
    load_sem, own_sem, piece_recv, z_send, y_send, x_send, band_send, band_recv, known,
):
    band = lax.axis_index("band")
    col = lax.axis_index("col")
    x, y, z = col // 16, (col // 2) % 8, col % 2
    mate = col + 1 - 2 * z
    z_peer = (band, mate)
    y_peers = {s: (band, 16 * x + 2 * ((y + s) % 8) + z) for s in NEAR_FIRST}
    x_peers = [(band, 16 * ((x + s) % 4) + 2 * y + z) for s in (1, 3, 2)]
    band_peers = [((band + s) % BANDS, col) for s in range(1, BANDS)]

    barrier = pltpu.get_barrier_semaphore()
    level = band // 2

    def near(step, act):
        for sign in (-1, 1):

            @pl.when((level + sign * step >= 0) & (level + sign * step < BANDS // 2))
            def _():
                act((band + 2 * sign * step, col))

    def beside(step):
        return jnp.where(level >= step, 1, 0) + jnp.where(level < BANDS // 2 - step, 1, 0)

    def call(semaphore, peer):
        pl.semaphore_signal(semaphore, inc=1, device_id=peer, device_id_type=MESH)

    core_peer = (band + 1 - 2 * (band % 2), col)
    @pl.when(z == 0)
    def _():
        call(barrier, z_peer)

    for peer in list(y_peers.values()) + x_peers + [core_peer]:
        call(barrier, peer)
    near(1, lambda peer: call(barrier, peer))
    loads = [
        pltpu.make_async_copy(source, target, load_sem.at[i])
        for i, (source, target) in enumerate(
            [(waves_hbm, waves_ref), (coup_hbm, coup_ref), (tend_hbm, tend_ref)]
        )
    ]
    for load in loads:
        load.start()
    keep = pltpu.make_async_copy(traj_hbm, piece_ref.at[col], own_sem)
    keep.start()
    pl.semaphore_wait(barrier, 11 + beside(1) + z)

    sent = []

    def send(source, slot, send_sem, peer):
        copy = pltpu.make_async_remote_copy(
            src_ref=source,
            dst_ref=piece_ref.at[slot],
            send_sem=send_sem,
            recv_sem=piece_recv.at[slot],
            device_id=peer,
            device_id_type=MESH,
        )
        copy.start()
        sent.append(copy)

    def arrive(slot):
        pltpu.make_async_remote_copy(
            src_ref=piece_ref.at[slot],
            dst_ref=piece_ref.at[slot],
            send_sem=z_send,
            recv_sem=piece_recv.at[slot],
            device_id=z_peer,
            device_id_type=MESH,
        ).wait_recv()

    def along(source, slot, own):
        for s in (1, 7, 4, 2, 6, 3, 5):
            send(source, slot, y_send.at[own, s], y_peers[s])

    def across(source, slot, own, s):
        for k, peer in enumerate(x_peers):
            send(source, slot, x_send.at[own, s, k], peer)

    exchange = pltpu.make_async_remote_copy(
        src_ref=traj_hbm,
        dst_ref=piece_ref.at[col],
        send_sem=z_send,
        recv_sem=piece_recv.at[col],
        device_id=z_peer,
        device_id_type=MESH,
    )
    sent.append(exchange)

    @pl.when(z == 1)
    def _():
        exchange.start()

    along(traj_hbm, col, 0)
    across(traj_hbm, col, 0, 0)
    near(1, lambda peer: call(known.at[0], peer))

    def pass_on(zz, own, offsets):
        for s in offsets:
            slot = 16 * x + 2 * ((y + s) % 8) + zz
            arrive(slot)
            across(piece_ref.at[slot], slot, own, s)

    loads[0].wait()
    latitude = lat_ref[0]
    points = jnp.minimum(20 + 4 * jnp.minimum(latitude, LATITUDES - 1 - latitude), POINTS)
    tables(points, waves_ref, fine_ref, a_ref, b_ref, range(3))
    pass_on(z, 0, NEAR_FIRST[:2])
    pl.semaphore_wait(known.at[0], beside(1))
    near(2, lambda peer: call(known.at[1], peer))
    tables(points, waves_ref, fine_ref, a_ref, b_ref, range(3, 6))
    pass_on(z, 0, NEAR_FIRST[2:4])
    for load in loads[1:]:
        load.wait()
    ratio = (2.0 * jnp.full((8, 128), latitude.astype(jnp.float32)) + 1.0) / LATITUDES
    turning = sine_turns(0.25 - 0.25 * ratio)
    back = coup_ref[...].astype(jnp.float32).T.astype(jnp.bfloat16)
    back_ref[...] = jnp.concatenate([back, back], axis=1)
    for zz in range(2):
        fine_ref[zz, PIECE:] = jnp.zeros((128 - PIECE, LANES), jnp.bfloat16)

    def two(xp, carry):
        repack(tend_ref, block_ref, xp)
        return carry

    lax.fori_loop(0, 4, two, 0)
    keep.wait()

    def add(xp, zz, first):
        column(turning, points, block_ref, piece_ref, coup_ref, back_ref, x_ref, xp, zz)

        def tile(j, carry):
            u, v = transform(x_ref, fine_ref, a_ref, b_ref, xp, zz, j)
            if not first:
                u = u + u_ref[j]
                v = v + v_ref[j]
            u_ref[j] = u
            v_ref[j] = v
            return carry

        lax.fori_loop(0, 6, tile, 0, unroll=True)

    def take(xp, zz):
        for k in range(8):
            arrive(16 * xp + 2 * k + zz)

    pass_on(z, 0, NEAR_FIRST[4:])
    pl.semaphore_wait(known.at[1], beside(2))
    near(1, lambda peer: call(known.at[2], peer))
    add(x, z, True)
    arrive(mate)
    along(piece_ref.at[mate], mate, 1)
    across(piece_ref.at[mate], mate, 1, 0)

    @pl.when(z == 0)
    def _():
        exchange.start()


    take((x + 1) % 4, z)
    add((x + 1) % 4, z, False)
    take((x + 3) % 4, z)
    add((x + 3) % 4, z, False)
    take((x + 2) % 4, z)
    add((x + 2) % 4, z, False)
    pl.semaphore_wait(known.at[2], beside(1))
    call(known.at[3], core_peer)
    pass_on(1 - z, 1, NEAR_FIRST[:])
    add(x, 1 - z, False)
    for s in (1, 3):
        take((x + s) % 4, 1 - z)
        add((x + s) % 4, 1 - z, False)

    pl.semaphore_wait(known.at[3], 1)
    xp, zz = (x + 2) % 4, 1 - z
    take(xp, zz)
    column(turning, points, block_ref, piece_ref, coup_ref, back_ref, x_ref, xp, zz)

    def unpack(row, ref):
        both = ref[row].astype(jnp.float32)
        out_ref[0, row] = both[:, :OWN_WAVES].astype(jnp.bfloat16)
        out_ref[1, row] = both[:, OWN_WAVES:].astype(jnp.bfloat16)


    def to_band(d):
        return pltpu.make_async_remote_copy(
            src_ref=send_ref.at[d],
            dst_ref=part_ref.at[band],
            send_sem=band_send.at[d],
            recv_sem=band_recv.at[band],
            device_id=(d, col),
            device_id_type=MESH,
        )

    def last(s, carry):
        j = jnp.where(band >= BANDS // 2, s, BANDS // 2 - 1 - s)
        u, v = transform(x_ref, fine_ref, a_ref, b_ref, xp, zz, j)
        u = u + u_ref[j]
        v = v + v_ref[j]
        for odd in range(2):
            d = 2 * j + odd
            half = slice(128 * odd, 128 * odd + 128)
            send_ref[d] = (u[:, half] + pltpu.roll(v[:, half], 64, 1)).astype(jnp.bfloat16)

            @pl.when(d != band)
            def _():
                to_band(d).start()

        return carry

    lax.fori_loop(0, 6, last, 0, unroll=True)
    unpack(band, send_ref)
    for copy in sent:
        copy.wait_send()
    for s in range(1, BANDS):
        source = (band + s) % BANDS
        pltpu.make_async_remote_copy(
            src_ref=send_ref.at[source],
            dst_ref=part_ref.at[source],
            send_sem=band_send.at[source],
            recv_sem=band_recv.at[source],
            device_id=band_peers[0],
            device_id_type=MESH,
        ).wait_recv()
        unpack(source, part_ref)
    for s in range(1, BANDS):
        to_band((band + s) % BANDS).wait_send()


def body(adjoint_tend, trajectory, coupling, row_lat, row_points, wave_order):
    vmem, smem, dma = pltpu.VMEM, pltpu.SMEM, pltpu.SemaphoreType.DMA
    arrays = [
        pltpu.with_memory_space_constraint(array, pltpu.HBM)
        for array in (adjoint_tend[0, :, 0, :], trajectory[:, 0, :], coupling, wave_order)
    ]
    parts = pl.pallas_call(
        kernel,
        out_shape=jax.ShapeDtypeStruct((2, BANDS, VARS, OWN_WAVES), jnp.bfloat16),
        in_specs=[pl.BlockSpec(memory_space=smem)] + [pl.BlockSpec(memory_space=pltpu.HBM)] * 4,
        out_specs=pl.BlockSpec(memory_space=vmem),
        scratch_shapes=[
            vmem((VARS, VARS), jnp.bfloat16),
            vmem((VARS, 2 * VARS), jnp.bfloat16),
            vmem((WAVES,), jnp.int32),
            vmem((VARS, POINTS), jnp.bfloat16),
            vmem((8, VARS, 1024), jnp.float32),
            vmem((64, VARS, PIECE), jnp.bfloat16),
            vmem((2, 128, LANES), jnp.bfloat16),
            vmem((32, LANES), jnp.float32),
            vmem((32, LANES), jnp.float32),
            vmem((8 * VARS, 128), jnp.bfloat16),
            vmem((6, VARS, 256), jnp.float32),
            vmem((6, VARS, 256), jnp.float32),
            vmem((BANDS, VARS, 128), jnp.bfloat16),
            vmem((BANDS, VARS, 128), jnp.bfloat16),
            dma((3,)),
            dma,
            dma((64,)),
            dma,
            dma((2, 8)),
            dma((2, 8, 3)),
            dma((BANDS,)),
            dma((BANDS,)),
            pltpu.SemaphoreType.REGULAR((4,)),
        ],
        compiler_params=pltpu.CompilerParams(
            vmem_limit_bytes=32 << 20, collective_id=0, has_side_effects=True
        ),
    )(row_lat, *arrays)
    return parts.transpose(0, 2, 1, 3)[None]


def solution(mesh):
    return jax.shard_map(
        body,
        mesh=mesh,
        in_specs=(
            P("col", None, "band", None),
            P(None, "band", "col"),
            P(),
            P("band"),
            P("band"),
            P(),
        ),
        out_specs=P("col", None, None, None, "band"),
        check_vma=False,
    )
```

```python
import jax
import jax.numpy as jnp
from jax import lax
from jax.experimental import pallas as pl
from jax.experimental.pallas import tpu as pltpu
from jax.sharding import PartitionSpec as P

LEVELS = 8
LATITUDES = 2560
VARS = 40
POINTS = 5120
WAVES = 768
PIECE = 80
BANDS = 12
OWN_WAVES = 64
LANES = 2 * BANDS * OWN_WAVES
STEP = 2 * PIECE
SINE = (6.283185005187988, -41.34165573120117, 81.60100555419922, -76.5497817993164, 39.536705017089844)
MESH = pl.DeviceIdType.MESH
NEAR_FIRST = (1, 7, 2, 6, 3, 5, 4)


def sine_turns(v):
    u = v * v
    p = jnp.full_like(u, SINE[-1])
    for c in SINE[-2::-1]:
        p = p * u + c
    return p * v


def cosine_turns(t):
    v = 0.25 - jnp.abs(t)
    return sine_turns(jnp.maximum(v, -0.5 - v))


def turns(pm, n, rn):
    q = jnp.floor(pm * rn + 0.5)
    return (pm - q * n) * rn


def tables(points, waves_ref, fine_ref, a_ref, b_ref, chosen):
    lane = lax.broadcasted_iota(jnp.int32, (8, 128), 1)
    first_half = lane < 64
    n8 = jnp.full((8, 128), points.astype(jnp.float32), jnp.float32)
    rn8 = 1.0 / n8
    root8 = 1.0 / jnp.sqrt(n8)
    shift8 = jnp.where(first_half, 0.0, 0.25)
    sign8 = jnp.where(first_half, 1.0, -1.0)
    row8 = lax.broadcasted_iota(jnp.int32, (8, 128), 0).astype(jnp.float32)
    for tile in chosen:
        pair = jnp.broadcast_to(waves_ref[pl.ds(128 * tile, 128)].reshape(1, 128), (8, 128)).astype(jnp.float32)
        turned = pltpu.roll(pair, 64, 1)
        for odd in range(2):
            w8 = jnp.where(first_half, pair, turned) if odd == 0 else jnp.where(first_half, turned, pair)
            at = (2 * tile + odd) * 128
            scale = jnp.where(2.0 * w8 < n8, root8, 0.0)
            for k in range(4):
                t = turns((row8 + 8.0 * k) * STEP * w8, n8, rn8)
                a_ref[8 * k : 8 * k + 8, at : at + 128] = scale * sign8 * cosine_turns(t)
                b_ref[8 * k : 8 * k + 8, at : at + 128] = -scale * cosine_turns(t - 0.25)
            wide = lambda v: jnp.broadcast_to(v[None], (PIECE // 8, 8, 128)).reshape(PIECE, 128)
            for zz in range(2):
                p0 = lax.broadcasted_iota(jnp.int32, (PIECE, 128), 0).astype(jnp.float32) + float(PIECE * zz)
                t = turns(p0 * wide(w8), wide(n8), wide(rn8))
                fine_ref[zz, 0:PIECE, at : at + 128] = cosine_turns(t - wide(shift8)).astype(jnp.bfloat16)


def repack(tend_ref, block_ref, xp):
    lane = lax.broadcasted_iota(jnp.int32, (VARS, 128), 1)
    for zz in range(2):
        for y in range(8):
            tile, at = divmod(STEP * y + PIECE * zz, 128)

            def load(k):
                start = pl.multiple_of(xp * 1280 + 128 * k, 128)
                return pltpu.roll(tend_ref[:, pl.ds(start, 128)].astype(jnp.float32), (128 - at) % 128, 1)

            piece = load(tile)
            if at + PIECE > 128:
                piece = jnp.where(lane < 128 - at, piece, load(tile + 1))
            block_ref[2 * xp + zz, :, 128 * y : 128 * y + 128] = piece


def column(turning, points, block_ref, piece_ref, coup_ref, back_ref, x_ref, xp, zz):
    zeros = jnp.zeros((VARS, 128 - PIECE), jnp.float32)
    pieces = [piece_ref[16 * xp + 2 * y + zz].astype(jnp.float32) for y in range(8)]
    traj = jnp.concatenate([part for piece in pieces for part in (piece, zeros)], axis=1)
    tend = block_ref[2 * xp + zz]
    driven = jnp.dot(coup_ref[...], traj.astype(jnp.bfloat16), preferred_element_type=jnp.float32)
    weighted = tend * (1.0 + traj)
    high = weighted.astype(jnp.bfloat16).astype(jnp.float32)
    both = jnp.concatenate([high, weighted - high], axis=0).astype(jnp.bfloat16)
    backed = jnp.dot(back_ref[...], both, preferred_element_type=jnp.float32)
    total = backed + tend * driven
    turn = jnp.tile(turning, (1, 8))
    total = jnp.concatenate(
        [
            total[:LEVELS] - turn * tend[LEVELS : 2 * LEVELS],
            total[LEVELS : 2 * LEVELS] + turn * tend[:LEVELS],
            total[2 * LEVELS :],
        ],
        axis=0,
    )
    q = lax.broadcasted_iota(jnp.int32, (VARS, 128), 1)
    first = xp * 1280 + zz * PIECE
    rows = []
    for y in range(8):
        keep = (q < PIECE) & (q + (first + STEP * y) < points)
        rows.append(jnp.where(keep, total[:, 128 * y : 128 * y + 128], 0.0))
    x_ref[...] = jnp.concatenate(rows, axis=0).astype(jnp.bfloat16)


def transform(x_ref, fine_ref, a_ref, b_ref, xp, zz, j):
    at = pl.multiple_of(j * 256, 256)
    y = jnp.dot(x_ref[...], fine_ref[zz, :, pl.ds(at, 256)], preferred_element_type=jnp.float32)
    a = a_ref[pl.ds(pl.multiple_of(8 * xp, 8), 8), pl.ds(at, 256)]
    b = b_ref[pl.ds(pl.multiple_of(8 * xp, 8), 8), pl.ds(at, 256)]
    u = y[:VARS] * a[0:1]
    v = y[:VARS] * b[0:1]
    for k in range(1, 8):
        part = y[VARS * k : VARS * (k + 1)]
        u = u + part * a[k : k + 1]
        v = v + part * b[k : k + 1]
    return u, v


def kernel(
    lat_ref, tend_hbm, traj_hbm, coup_hbm, waves_hbm, out_ref,
    coup_ref, back_ref, waves_ref, tend_ref, block_ref, piece_ref,
    fine_ref, a_ref, b_ref, x_ref, u_ref, v_ref, send_ref, part_ref,
    load_sem, own_sem, piece_recv, z_send, y_send, x_send, band_send, band_recv, known,
):
    band = lax.axis_index("band")
    col = lax.axis_index("col")
    x, y, z = col // 16, (col // 2) % 8, col % 2
    mate = col + 1 - 2 * z
    z_peer = (band, mate)
    y_peers = {s: (band, 16 * x + 2 * ((y + s) % 8) + z) for s in NEAR_FIRST}
    x_peers = [(band, 16 * ((x + s) % 4) + 2 * y + z) for s in (2, 1, 3)]
    band_peers = [((band + s) % BANDS, col) for s in range(1, BANDS)]

    barrier = pltpu.get_barrier_semaphore()
    level = band // 2

    def near(step, act):
        for sign in (-1, 1):

            @pl.when((level + sign * step >= 0) & (level + sign * step < BANDS // 2))
            def _():
                act((band + 2 * sign * step, col))

    def beside(step):
        return jnp.where(level >= step, 1, 0) + jnp.where(level < BANDS // 2 - step, 1, 0)

    def call(semaphore, peer):
        pl.semaphore_signal(semaphore, inc=1, device_id=peer, device_id_type=MESH)

    core_peer = (band + 1 - 2 * (band % 2), col)
    @pl.when(z == 0)
    def _():
        call(barrier, z_peer)

    for peer in list(y_peers.values()) + x_peers + [core_peer]:
        call(barrier, peer)
    near(1, lambda peer: call(barrier, peer))
    loads = [
        pltpu.make_async_copy(source, target, load_sem.at[i])
        for i, (source, target) in enumerate(
            [(waves_hbm, waves_ref), (coup_hbm, coup_ref), (tend_hbm, tend_ref)]
        )
    ]
    for load in loads:
        load.start()
    keep = pltpu.make_async_copy(traj_hbm, piece_ref.at[col], own_sem)
    keep.start()
    pl.semaphore_wait(barrier, 11 + beside(1) + z)

    sent = []

    def send(source, slot, send_sem, peer):
        copy = pltpu.make_async_remote_copy(
            src_ref=source,
            dst_ref=piece_ref.at[slot],
            send_sem=send_sem,
            recv_sem=piece_recv.at[slot],
            device_id=peer,
            device_id_type=MESH,
        )
        copy.start()
        sent.append(copy)

    def arrive(slot):
        pltpu.make_async_remote_copy(
            src_ref=piece_ref.at[slot],
            dst_ref=piece_ref.at[slot],
            send_sem=z_send,
            recv_sem=piece_recv.at[slot],
            device_id=z_peer,
            device_id_type=MESH,
        ).wait_recv()

    def along(source, slot, own):
        for s in (1, 7, 4, 2, 6, 3, 5):
            send(source, slot, y_send.at[own, s], y_peers[s])

    def across(source, slot, own, s):
        for k, peer in enumerate(x_peers):
            send(source, slot, x_send.at[own, s, k], peer)

    exchange = pltpu.make_async_remote_copy(
        src_ref=traj_hbm,
        dst_ref=piece_ref.at[col],
        send_sem=z_send,
        recv_sem=piece_recv.at[col],
        device_id=z_peer,
        device_id_type=MESH,
    )
    sent.append(exchange)

    @pl.when(z == 1)
    def _():
        exchange.start()

    along(traj_hbm, col, 0)
    across(traj_hbm, col, 0, 0)
    near(1, lambda peer: call(known.at[0], peer))

    def pass_on(zz, own, offsets):
        for s in offsets:
            slot = 16 * x + 2 * ((y + s) % 8) + zz
            arrive(slot)
            across(piece_ref.at[slot], slot, own, s)

    loads[0].wait()
    latitude = lat_ref[0]
    points = jnp.minimum(20 + 4 * jnp.minimum(latitude, LATITUDES - 1 - latitude), POINTS)
    tables(points, waves_ref, fine_ref, a_ref, b_ref, range(3))
    pass_on(z, 0, NEAR_FIRST[:2])
    pl.semaphore_wait(known.at[0], beside(1))
    near(2, lambda peer: call(known.at[1], peer))
    tables(points, waves_ref, fine_ref, a_ref, b_ref, range(3, 6))
    pass_on(z, 0, NEAR_FIRST[2:4])
    for load in loads[1:]:
        load.wait()
    ratio = (2.0 * jnp.full((8, 128), latitude.astype(jnp.float32)) + 1.0) / LATITUDES
    turning = sine_turns(0.25 - 0.25 * ratio)
    back = coup_ref[...].astype(jnp.float32).T.astype(jnp.bfloat16)
    back_ref[...] = jnp.concatenate([back, back], axis=1)
    for zz in range(2):
        fine_ref[zz, PIECE:] = jnp.zeros((128 - PIECE, LANES), jnp.bfloat16)

    def two(xp, carry):
        repack(tend_ref, block_ref, xp)
        return carry

    lax.fori_loop(0, 4, two, 0)
    keep.wait()

    def add(xp, zz, first):
        column(turning, points, block_ref, piece_ref, coup_ref, back_ref, x_ref, xp, zz)

        def tile(j, carry):
            u, v = transform(x_ref, fine_ref, a_ref, b_ref, xp, zz, j)
            if not first:
                u = u + u_ref[j]
                v = v + v_ref[j]
            u_ref[j] = u
            v_ref[j] = v
            return carry

        lax.fori_loop(0, 6, tile, 0, unroll=True)

    def take(xp, zz):
        for k in range(8):
            arrive(16 * xp + 2 * k + zz)

    pass_on(z, 0, NEAR_FIRST[4:])
    pl.semaphore_wait(known.at[1], beside(2))
    near(1, lambda peer: call(known.at[2], peer))
    add(x, z, True)
    arrive(mate)
    along(piece_ref.at[mate], mate, 1)
    across(piece_ref.at[mate], mate, 1, 0)

    @pl.when(z == 0)
    def _():
        exchange.start()


    take((x + 1) % 4, z)
    add((x + 1) % 4, z, False)
    take((x + 3) % 4, z)
    add((x + 3) % 4, z, False)
    take((x + 2) % 4, z)
    add((x + 2) % 4, z, False)
    pl.semaphore_wait(known.at[2], beside(1))
    call(known.at[3], core_peer)
    pass_on(1 - z, 1, NEAR_FIRST[:])
    add(x, 1 - z, False)
    for s in (1, 3):
        take((x + s) % 4, 1 - z)
        add((x + s) % 4, 1 - z, False)

    pl.semaphore_wait(known.at[3], 1)
    xp, zz = (x + 2) % 4, 1 - z
    take(xp, zz)
    column(turning, points, block_ref, piece_ref, coup_ref, back_ref, x_ref, xp, zz)

    def unpack(row, ref):
        both = ref[row].astype(jnp.float32)
        out_ref[0, row] = both[:, :OWN_WAVES].astype(jnp.bfloat16)
        out_ref[1, row] = both[:, OWN_WAVES:].astype(jnp.bfloat16)


    def to_band(d):
        return pltpu.make_async_remote_copy(
            src_ref=send_ref.at[d],
            dst_ref=part_ref.at[band],
            send_sem=band_send.at[d],
            recv_sem=band_recv.at[band],
            device_id=(d, col),
            device_id_type=MESH,
        )

    def last(s, carry):
        j = jnp.where(band >= BANDS // 2, s, BANDS // 2 - 1 - s)
        u, v = transform(x_ref, fine_ref, a_ref, b_ref, xp, zz, j)
        u = u + u_ref[j]
        v = v + v_ref[j]
        for odd in range(2):
            d = 2 * j + odd
            half = slice(128 * odd, 128 * odd + 128)
            send_ref[d] = (u[:, half] + pltpu.roll(v[:, half], 64, 1)).astype(jnp.bfloat16)

            @pl.when(d != band)
            def _():
                to_band(d).start()

        return carry

    lax.fori_loop(0, 6, last, 0, unroll=True)
    unpack(band, send_ref)
    for copy in sent:
        copy.wait_send()
    for s in range(1, BANDS):
        source = (band + s) % BANDS
        pltpu.make_async_remote_copy(
            src_ref=send_ref.at[source],
            dst_ref=part_ref.at[source],
            send_sem=band_send.at[source],
            recv_sem=band_recv.at[source],
            device_id=band_peers[0],
            device_id_type=MESH,
        ).wait_recv()
        unpack(source, part_ref)
    for s in range(1, BANDS):
        to_band((band + s) % BANDS).wait_send()


def body(adjoint_tend, trajectory, coupling, row_lat, row_points, wave_order):
    vmem, smem, dma = pltpu.VMEM, pltpu.SMEM, pltpu.SemaphoreType.DMA
    arrays = [
        pltpu.with_memory_space_constraint(array, pltpu.HBM)
        for array in (adjoint_tend[0, :, 0, :], trajectory[:, 0, :], coupling, wave_order)
    ]
    parts = pl.pallas_call(
        kernel,
        out_shape=jax.ShapeDtypeStruct((2, BANDS, VARS, OWN_WAVES), jnp.bfloat16),
        in_specs=[pl.BlockSpec(memory_space=smem)] + [pl.BlockSpec(memory_space=pltpu.HBM)] * 4,
        out_specs=pl.BlockSpec(memory_space=vmem),
        scratch_shapes=[
            vmem((VARS, VARS), jnp.bfloat16),
            vmem((VARS, 2 * VARS), jnp.bfloat16),
            vmem((WAVES,), jnp.int32),
            vmem((VARS, POINTS), jnp.bfloat16),
            vmem((8, VARS, 1024), jnp.float32),
            vmem((64, VARS, PIECE), jnp.bfloat16),
            vmem((2, 128, LANES), jnp.bfloat16),
            vmem((32, LANES), jnp.float32),
            vmem((32, LANES), jnp.float32),
            vmem((8 * VARS, 128), jnp.bfloat16),
            vmem((6, VARS, 256), jnp.float32),
            vmem((6, VARS, 256), jnp.float32),
            vmem((BANDS, VARS, 128), jnp.bfloat16),
            vmem((BANDS, VARS, 128), jnp.bfloat16),
            dma((3,)),
            dma,
            dma((64,)),
            dma,
            dma((2, 8)),
            dma((2, 8, 3)),
            dma((BANDS,)),
            dma((BANDS,)),
            pltpu.SemaphoreType.REGULAR((4,)),
        ],
        compiler_params=pltpu.CompilerParams(
            vmem_limit_bytes=32 << 20, collective_id=0, has_side_effects=True
        ),
    )(row_lat, *arrays)
    return parts.transpose(0, 2, 1, 3)[None]


def solution(mesh):
    return jax.shard_map(
        body,
        mesh=mesh,
        in_specs=(
            P("col", None, "band", None),
            P(None, "band", "col"),
            P(),
            P("band"),
            P("band"),
            P(),
        ),
        out_specs=P("col", None, None, None, "band"),
        check_vma=False,
    )
```
